32 devices in a mesh: round: 2 (over x), brick: 16 (over z, y, core).
Axes of the slice: x: 2, y: 2, z: 4, core: 2. Of those that a mesh axis runs over, the one named last changes fastest.
Arguments:
- image: bfloat16 [2, 128, 4, 32, 8, 128], P('round', 'brick'), may hold values from -60 to 60
- shifts: int32 [2, 128], P('round', 'brick'), may hold values from -24 to 24, as said below
- fractions: float32 [2, 128], P('round', 'brick'), may hold values from 0 to 1
- valid: int32 [128], replicated, may hold values from 0 to 1, as said below
Outputs:
- spots: bfloat16 [2, 2, 64, 4, 32, 8, 128], P(None, 'round', 'brick')
The draws below stay inside these ranges and needn't reach their ends.
Inputs may be any that keep to these rules, and one draw needn't show every extreme that they name: `shifts`: in every round, the last brick of each aligned block of 8 bricks has a shift between minus 24 and minus half of 24 (rounded down), and the first brick of each such block a shift between half of 24 (rounded down) and 24. `valid`: the first and the last brick of each aligned block of 8 bricks hold tissue.
All inputs are finite; a program needn't handle non-finite values.
Results may differ from the reference program's by a relative error of at most 0.0055.
Values may be sent and summed in bfloat16 or wider, within the bound.
No kernel may reach another device: no remote copies, remote signals or barrier semaphores. Data moves between devices by JAX's collectives and lax.ppermute only.
A program may use at most 128 MiB of HBM per device.

```python
import jax
import jax.numpy as jnp
from jax import lax

CHANNELS = 4
DEPTH = 32
HEIGHT = 8
WIDTH = 128
SMAX = 24
BRK_DEV = 8
ROUNDS = 2
BRICKS = 128
N_ROUND = 2
N_BRICK = 16


def draw_image(key, part):
    first, second = jax.random.split(jax.random.fold_in(key, 11))
    shape = (ROUNDS, BRICKS, CHANNELS, DEPTH, HEIGHT, WIDTH)
    rise = 1.0 + 2.0 * jnp.arange(BRICKS, dtype=jnp.float32) / max(BRICKS - 1, 1)
    noise = jnp.clip(jax.random.normal(first, shape, jnp.float32), -6.0, 6.0)
    plane = jnp.exp(jax.random.uniform(second, (ROUNDS, BRICKS, CHANNELS, 1, HEIGHT, 1), jnp.float32, 0.0, 1.098612))
    values = noise * plane * rise[None, :, None, None, None, None]
    return values.astype(jnp.bfloat16)


def draw_shifts(key, part):
    common = jax.random.randint(jax.random.fold_in(key, 21), (ROUNDS, BRICKS), 0 - SMAX, SMAX + 1)
    strong = jax.random.randint(jax.random.fold_in(key, 22), (ROUNDS, BRICKS), SMAX // 2, SMAX + 1)
    position = jnp.arange(BRICKS, dtype=jnp.int32) % BRK_DEV
    result = jnp.where(position[None, :] == BRK_DEV - 1, 0 - strong, common)
    result = jnp.where(position[None, :] == 0, strong, result)
    return result.astype(jnp.int32)


def draw_valid(key, part):
    pick = jax.random.randint(jax.random.fold_in(key, 31), (BRICKS,), 0, 4)
    position = jnp.arange(BRICKS, dtype=jnp.int32) % BRK_DEV
    edge = (position == 0) | (position == BRK_DEV - 1)
    return jnp.where(edge | (pick < 3), 1, 0).astype(jnp.int32)


def level_of(rng, dims, pieces, least, high):
    def one(dim, blocks):
        steps = jax.random.uniform(jax.random.fold_in(jax.random.fold_in(rng, 6), dim), (blocks,), jnp.float32, least / len(pieces), high / len(pieces))
        return jnp.repeat(jnp.exp(steps), dims[dim] // blocks).reshape((-1,) + (1,) * (len(dims) - dim - 1))

    factor_of = one(*pieces[0])
    for cut in pieces[1:]:
        factor_of = factor_of * one(*cut)
    return factor_of


def setup_inputs(seed: int = 0) -> dict:
    key_of = jax.random.split(jax.random.key(seed), 5)
    return {
        "image": draw_image(jax.random.fold_in(key_of[4], 71), 0),
        "shifts": draw_shifts(jax.random.fold_in(key_of[4], 71), 0),
        "fractions": jnp.clip(1.0 * jax.random.uniform(key_of[2], (ROUNDS, BRICKS), jnp.float32) ** level_of(key_of[2], (ROUNDS, BRICKS), ((0, 2), (1, 16)), -0.2, 0.2), 0.0, 1.0),
        "valid": draw_valid(jax.random.fold_in(key_of[4], 71), 0),
    }


sigma_spot = 1.5

def kernel_tables(count):
    index = jnp.arange(count, dtype=jnp.float32)
    offset = index[:, None] - index[None, :]
    smooth = jnp.exp(-offset * offset / (2.0 * sigma_spot * sigma_spot)) / (2.5066282746310002 * sigma_spot)
    smooth = jnp.where(jnp.abs(offset) < 4.0 * sigma_spot, smooth, jnp.float32(0.0))
    curve = (offset * offset / sigma_spot ** 4 - 1.0 / sigma_spot ** 2) * smooth
    return (smooth, curve)

def spot_filter(field):
    values = field.astype(jnp.float32)
    depth, height, width = field.shape[-3:]
    gauss_z, curve_z = kernel_tables(depth)
    gauss_y, curve_y = kernel_tables(height)
    gauss_x, curve_x = kernel_tables(width)
    high = lax.Precision.HIGHEST
    along_x = jnp.einsum('...x,wx->...w', values, gauss_x, precision=high)
    bent_x = jnp.einsum('...x,wx->...w', values, curve_x, precision=high)
    plain_y = jnp.einsum('...yx,vy->...vx', along_x, gauss_y, precision=high)
    bent_y = jnp.einsum('...yx,vy->...vx', along_x, curve_y, precision=high)
    mixed_y = jnp.einsum('...yx,vy->...vx', bent_x, gauss_y, precision=high)
    outer = jnp.einsum('...zyx,wz->...wyx', mixed_y + bent_y, gauss_z, precision=high)
    outer = outer + jnp.einsum('...zyx,wz->...wyx', plain_y, curve_z, precision=high)
    return (-(sigma_spot * sigma_spot) * outer).astype(jnp.bfloat16)

def shift_strip(padded, offsets, fraction_row, width):

    def one_brick(start, fraction):
        window = lax.dynamic_slice_in_dim(padded, start, width + 1, padded.ndim - 1).astype(jnp.float32)
        return ((1.0 - fraction) * window[..., 1:] + fraction * window[..., :-1]).astype(jnp.bfloat16)
    return jax.vmap(one_brick)(offsets, fraction_row)

def reference(image, shifts, fractions, valid):
    depth, height, width = image.shape[-3:]
    bricks = image.shape[1]
    reach = SMAX + 1
    weights = valid.astype(jnp.bfloat16)
    masked = image * weights[None, :, None, None, None, None]

    def per_round(items):
        layer, shift_row, fraction_row = items
        strip = jnp.moveaxis(layer, 0, 3).reshape(layer.shape[1], depth, height, bricks * width)
        padded = jnp.pad(strip, ((0, 0), (0, 0), (0, 0), (reach, reach)))
        offsets = (jnp.arange(bricks, dtype=jnp.int32) * width + reach - shift_row - 1).astype(jnp.int32)
        shifted = shift_strip(padded, offsets, fraction_row, width)
        filtered = spot_filter(shifted)
        magnitude = lax.optimization_barrier(jnp.sum(jnp.abs(filtered.astype(jnp.float32)), axis=(2, 3, 4)))
        total = lax.optimization_barrier(jnp.sum(magnitude * valid.astype(jnp.float32)[:, None], axis=0))
        return (filtered, total)
    filtered, total = lax.map(per_round, (masked, shifts, fractions))
    count = jnp.maximum(jnp.sum(valid).astype(jnp.float32), 1.0)
    scale = total / (count * depth * height * width) + 1e-06

    def per_brick(block):
        ratio = block.astype(jnp.float32) / scale[:, :, None, None, None]
        energy = lax.optimization_barrier(jnp.mean(ratio * ratio, axis=(0, 1), keepdims=True))
        return (ratio / jnp.sqrt(energy + 1.0)).astype(jnp.bfloat16)
    normed = lax.map(per_brick, jnp.moveaxis(filtered, 1, 0))
    rounds = image.shape[0]
    quarter = BRK_DEV // N_ROUND
    tail = normed.shape[2:]
    arranged = normed.reshape((N_BRICK, N_ROUND, quarter, rounds) + tail)
    arranged = jnp.transpose(arranged, (3, 1, 0, 2, 4, 5, 6, 7))
    return arranged.reshape((rounds, N_ROUND, N_BRICK * quarter) + tail)
```

```python
import functools

import jax
import jax.numpy as jnp
import numpy as np
from jax import lax
from jax.experimental import pallas as pl
from jax.experimental.pallas import tpu as pltpu
from jax.sharding import PartitionSpec as P

SMAX = 24

sigma_spot = 1.5

BF = jnp.bfloat16
F32 = jnp.float32
VMEM = pl.BlockSpec(memory_space=pltpu.VMEM)
SMEM = pl.BlockSpec(memory_space=pltpu.SMEM)


def kernel_tables(count):
    index = np.arange(count, dtype=np.float64)
    offset = index[:, None] - index[None, :]
    smooth = np.exp(-offset * offset / (2.0 * sigma_spot * sigma_spot)) / (
        2.5066282746310002 * sigma_spot
    )
    smooth = np.where(np.abs(offset) < 4.0 * sigma_spot, smooth, 0.0)
    curve = (offset * offset / sigma_spot**4 - 1.0 / sigma_spot**2) * smooth
    return smooth, curve


def split(table):
    table = np.asarray(table, np.float32)
    high = table.astype(BF)
    low = (table - high.astype(np.float32)).astype(BF)
    return np.stack([high, low])


def plane_tables(depth, height):
    gauss_z, curve_z = kernel_tables(depth)
    gauss_y, curve_y = kernel_tables(height)
    factor = -(sigma_spot * sigma_spot)
    with_bent = np.kron(gauss_z, gauss_y)
    with_smooth = np.kron(gauss_z, curve_y) + np.kron(curve_z, gauss_y)
    return split(factor * np.concatenate([with_bent, with_smooth], axis=0))


def line_tables(width):
    gauss_x, curve_x = kernel_tables(width)
    return np.stack([np.tile(t.T, (2, 1)) for t in (curve_x, gauss_x)]).astype(np.float32)


def lanes_of(shape):
    return lax.broadcasted_iota(jnp.int32, shape, len(shape) - 1)


def pack_kernel(valid_ref, img_ref, tail_ref, head_ref):
    bricks, channels, plane, width = img_ref.shape
    slot = width // channels
    first = lax.axis_index("brick") * bricks
    lane = lanes_of((plane, width))

    def pack(brick, at):
        row = jnp.zeros((plane, width), F32)
        for c in range(channels):
            data = img_ref[brick, c].astype(F32)
            amount = (c * slot - at) % width
            moved = pltpu.roll(data, amount, 1) if amount else data
            row = jnp.where(lane // slot == c, moved, row)
        return (row * valid_ref[first + brick].astype(F32)).astype(BF)

    tail_ref[...] = pack(bricks - 1, width - slot)
    head_ref[...] = pack(0, 0)


def filter_kernel(picks, edge, first_call, last_call, *refs):
    shift_ref, frac_ref, valid_ref, img_ref, plane_ref, line_ref = refs[:6]
    refs = refs[6:]
    if edge:
        tail_ref, head_ref = refs[:2]
        refs = refs[2:]
    if not first_call:
        sums_ref, refs = refs[0], refs[1:]
    out_ref, stat_ref = refs
    bricks, channels, plane, width = img_ref.shape
    slot = width // channels
    first = lax.axis_index("brick") * bricks
    rank = lax.axis_index("round")
    lane = lanes_of((1, width))
    totals = [jnp.zeros((8, width), F32) for _ in range(channels)]
    for n, pick in enumerate(picks):
        b = pick(rank)
        s = shift_ref[0, b]
        f = frac_ref[0, b]
        right = s >= 0
        nb = jnp.where(right, b - 1, b + 1)
        nb_in = jnp.clip(nb, 0, bricks - 1)
        own_valid = valid_ref[first + b].astype(F32)
        nb_valid = valid_ref[jnp.clip(first + nb, 0, valid_ref.shape[0] - 1)].astype(F32)
        if edge:
            nb_valid = jnp.where(nb == nb_in, nb_valid, 1.0)
        low0, high0 = jnp.where(right, 0, -s), jnp.where(right, width - s, width)
        low1, high1 = jnp.where(right, 0, -s - 1), jnp.where(right, width - s - 1, width)
        own0 = (lane >= low0) & (lane < high0)
        own1 = (lane >= low1) & (lane < high1)
        gain0 = (1.0 - f) * jnp.where(own0, own_valid, nb_valid)
        gain1 = f * jnp.where(own1, own_valid, nb_valid)
        own0, own1 = (jnp.broadcast_to(m, (plane, width)) for m in (own0, own1))
        parts = []
        for c in range(channels):
            own = img_ref[b, c].astype(F32)
            other = img_ref[nb_in, c].astype(F32)
            if edge:
                before = pltpu.roll(tail_ref[...].astype(F32), (width - slot - c * slot) % width, 1)
                after = head_ref[...].astype(F32)
                if c:
                    after = pltpu.roll(after, (width - c * slot) % width, 1)
                other = jnp.where(nb < 0, before, jnp.where(nb >= bricks, after, other))
            here = jnp.where(own0, own, other) * gain0
            there = jnp.where(own1, own, other) * gain1
            parts.append((here + pltpu.roll(there, 1, 1)).astype(BF))
        field = jnp.concatenate(parts, axis=1)
        dot = functools.partial(jnp.dot, preferred_element_type=F32)
        mixed = dot(plane_ref[0], field) + dot(plane_ref[1], field)
        turn = jnp.where(s < 0, s + width, s)
        line = jnp.concatenate([line_ref[k, pl.ds(turn, width), :] for k in range(2)], axis=0)
        line_high = line.astype(BF)
        line_low = (line - line_high.astype(F32)).astype(BF)
        for c in range(channels):
            wide = jnp.concatenate(
                [mixed[k * plane : (k + 1) * plane, c * width : (c + 1) * width] for k in range(2)],
                axis=1,
            )
            wide_high = wide.astype(BF)
            wide_low = (wide - wide_high.astype(F32)).astype(BF)
            result = dot(wide_high, line_high) + dot(wide_high, line_low) + dot(wide_low, line_high)
            result = result.astype(BF)
            out_ref[n, c] = result
            size = jnp.abs(result.astype(F32)).reshape(plane // 8, 8, width)
            totals[c] = totals[c] + jnp.sum(size, axis=0) * own_valid
    if not first_call:
        totals = [totals[c] + sums_ref[c] for c in range(channels)]
    if last_call:
        row = lax.broadcasted_iota(jnp.int32, (8, width), 0)
        packed = jnp.zeros((8, width), F32)
        for c in range(channels):
            packed = jnp.where(row == c, jnp.sum(totals[c]), packed)
        stat_ref[...] = packed
    else:
        for c in range(channels):
            stat_ref[c] = totals[c]


def norm_kernel(rounds, places, *refs):
    valid_ref, own_ref = refs[:2]
    stat_refs = refs[2 : 2 + rounds]
    chunk_refs = refs[2 + rounds : -1]
    out_ref = refs[-1]
    quota, channels, plane, width = own_ref.shape
    rank = lax.axis_index("round")
    count = jnp.maximum(jnp.sum(valid_ref[...]).astype(F32), 1.0)
    inverse = []
    for d in range(rounds):
        scale = stat_refs[d][...] / (count * (plane * width)) + 1e-06
        inverse.append(1.0 / scale)
    for j in range(quota):
        pos = jnp.where(rank == 0, quota - 1 - j, j)
        energy = jnp.zeros((plane, width), F32)
        values = []
        for d in range(rounds):
            for c in range(channels):
                data = own_ref[pos, c] if d == 0 else chunk_refs[places[d, j]][0, c]
                ratio = data.astype(F32) * inverse[d][c : c + 1, :]
                energy = energy + ratio * ratio
                values.append(ratio)
        factor = lax.rsqrt(energy * (1.0 / (rounds * channels)) + 1.0)
        for d in range(rounds):
            slot = jnp.where(rank >= d, rank - d, rank - d + rounds)
            for c in range(channels):
                out_ref[slot, 0, pos, c] = (values[d * channels + c] * factor).astype(BF)


def on_device(image, shifts, fractions, valid):
    _, bricks, channels, depth, height, width = image.shape
    plane = depth * height
    rounds = lax.axis_size("round")
    count = lax.axis_size("brick")
    quota = bricks // rounds
    img = image.reshape(bricks, channels, plane, width)
    plane_table = jnp.asarray(plane_tables(depth, height))
    line_table = jnp.asarray(line_tables(width))
    shape = jax.ShapeDtypeStruct

    tail, head = pl.pallas_call(
        pack_kernel,
        in_specs=[SMEM, VMEM],
        out_specs=[VMEM, VMEM],
        out_shape=[shape((plane, width), BF)] * 2,
        name="pack",
    )(valid, img)
    ends = count - 1
    before = lax.ppermute(tail, "brick", [(i, i + 1) for i in range(ends)])
    after = lax.ppermute(head, "brick", [(i + 1, i) for i in range(ends)])

    def pick_for(d, j):
        def pick(rank):
            target = (rank + d) % rounds
            return target * quota + jnp.where(target == 0, quota - 1 - j, j)

        return pick

    def own_pick(j):
        return lambda rank: rank * quota + j

    sums = None

    def filtered(picks, edge, last, sums):
        ins = [shifts, fractions, valid, img, plane_table, line_table]
        specs = [SMEM, SMEM, SMEM, VMEM, VMEM, VMEM]
        if edge:
            ins += [before, after]
            specs += [VMEM, VMEM]
        if sums is not None:
            ins.append(sums)
            specs.append(VMEM)
        stat = shape((8, width), F32) if last else shape((channels, 8, width), F32)
        return pl.pallas_call(
            functools.partial(filter_kernel, picks, edge, sums is None, last),
            in_specs=specs,
            out_specs=[VMEM, VMEM],
            out_shape=[shape((len(picks), channels, plane, width), BF), stat],
            name=f"filter{len(picks)}",
        )(*ins)

    places = {}
    chunks = []
    for j in range(quota):
        for d in range(1, rounds):
            edge = j == quota - 1
            part, sums = filtered([pick_for(d, j)], edge, False, sums)
            places[d, j] = len(chunks)
            chunks.append(lax.ppermute(part, "round", [(i, (i + d) % rounds) for i in range(rounds)]))
    own, stat = filtered([own_pick(j) for j in range(quota)], True, True, sums)

    step = 1
    while step < count:
        stat = stat + lax.ppermute(stat, "brick", [(i, i ^ step) for i in range(count)])
        step *= 2
    stats = [stat]
    for d in range(1, rounds):
        stats.append(lax.ppermute(stat, "round", [(i, (i + d) % rounds) for i in range(rounds)]))

    out = pl.pallas_call(
        functools.partial(norm_kernel, rounds, places),
        in_specs=[VMEM] * (2 + rounds + len(chunks)),
        out_specs=VMEM,
        out_shape=shape((rounds, 1, quota, channels, plane, width), BF),
        name="norm",
    )(valid.reshape(1, -1), own, *stats, *chunks)
    return out.reshape(rounds, 1, quota, channels, depth, height, width)


def solution(mesh):
    in_specs = (
        P("round", "brick", None, None, None, None),
        P("round", "brick"),
        P("round", "brick"),
        P(),
    )
    out_specs = P(None, "round", "brick", None, None, None, None)
    return jax.shard_map(
        on_device, mesh=mesh, in_specs=in_specs, out_specs=out_specs, check_vma=False
    )
```

```python
import functools

import jax
import jax.numpy as jnp
import numpy as np
from jax import lax
from jax.experimental import pallas as pl
from jax.experimental.pallas import tpu as pltpu
from jax.sharding import PartitionSpec as P

sigma_spot = 1.5


BF = jnp.bfloat16
F32 = jnp.float32
VMEM = pl.BlockSpec(memory_space=pltpu.VMEM)
SMEM = pl.BlockSpec(memory_space=pltpu.SMEM)
HBM = pl.BlockSpec(memory_space=pltpu.HBM)
PARAMS = pltpu.CompilerParams(vmem_limit_bytes=24 * 2**20)


def kernel_tables(count):
    index = np.arange(count, dtype=np.float64)
    offset = index[:, None] - index[None, :]
    smooth = np.exp(-offset * offset / (2.0 * sigma_spot * sigma_spot)) / (
        2.5066282746310002 * sigma_spot
    )
    smooth = np.where(np.abs(offset) < 4.0 * sigma_spot, smooth, 0.0)
    curve = (offset * offset / sigma_spot**4 - 1.0 / sigma_spot**2) * smooth
    return smooth, curve


def plane_tables(depth, height):
    gauss_z, curve_z = kernel_tables(depth)
    gauss_y, curve_y = kernel_tables(height)
    factor = -(sigma_spot * sigma_spot)
    with_bent = np.kron(gauss_z, gauss_y)
    with_smooth = np.kron(gauss_z, curve_y) + np.kron(curve_z, gauss_y)
    table = (factor * np.concatenate([with_bent, with_smooth], axis=0)).astype(np.float32)
    high = table.astype(BF)
    low = (table - high.astype(np.float32)).astype(BF)
    return np.concatenate([high, low], axis=0)


def line_tables(width):
    gauss_x, curve_x = kernel_tables(width)
    return np.stack([np.tile(t.T, (2, 1)) for t in (curve_x, gauss_x)]).astype(np.float32)


def lanes_of(shape):
    return lax.broadcasted_iota(jnp.int32, shape, len(shape) - 1)


def pack_kernel(valid_ref, img_ref, tail_ref, head_ref):
    bricks, channels, plane, width = img_ref.shape
    slot = width // channels
    first = lax.axis_index("brick") * bricks
    lane = lanes_of((plane, width))

    def pack(brick, at):
        row = jnp.zeros((plane, width), F32)
        for c in range(channels):
            data = img_ref[brick, c].astype(F32)
            amount = (c * slot - at) % width
            moved = pltpu.roll(data, amount, 1) if amount else data
            row = jnp.where(lane // slot == c, moved, row)
        return (row * valid_ref[first + brick].astype(F32)).astype(BF)

    tail_ref[...] = pack(bricks - 1, width - slot)
    head_ref[...] = pack(0, 0)


class Filter:
    def __init__(self, shift_ref, frac_ref, valid_ref, img_ref, plane_ref, line_ref, halo=None):
        self.shift, self.frac, self.valid = shift_ref, frac_ref, valid_ref
        self.img, self.plane, self.line, self.halo = img_ref, plane_ref, line_ref, halo

    def __call__(self, b, put, totals):
        bricks, channels, plane, width = self.img.shape
        slot = width // channels
        first = lax.axis_index("brick") * bricks
        lane = lanes_of((1, width))
        s = self.shift[0, b]
        f = self.frac[0, b]
        right = s >= 0
        nb = jnp.where(right, b - 1, b + 1)
        nb_in = jnp.clip(nb, 0, bricks - 1)
        own_valid = self.valid[first + b].astype(F32)
        nb_valid = self.valid[first + nb_in].astype(F32)
        if self.halo:
            nb_valid = jnp.where(nb == nb_in, nb_valid, 1.0)
        low0, high0 = jnp.where(right, 0, -s), jnp.where(right, width - s, width)
        low1, high1 = jnp.where(right, 0, -s - 1), jnp.where(right, width - s - 1, width)
        own0 = (lane >= low0) & (lane < high0)
        own1 = (lane >= low1) & (lane < high1)
        gain0 = (1.0 - f) * jnp.where(own0, own_valid, nb_valid)
        gain1 = f * jnp.where(own1, own_valid, nb_valid)
        own0, own1 = (jnp.broadcast_to(m, (plane, width)) for m in (own0, own1))
        parts = []
        for c in range(channels):
            own = self.img[b, c].astype(F32)
            other = self.img[nb_in, c].astype(F32)
            if self.halo:
                tail_ref, head_ref = self.halo
                before = pltpu.roll(tail_ref[...].astype(F32), (width - slot - c * slot) % width, 1)
                after = head_ref[...].astype(F32)
                if c:
                    after = pltpu.roll(after, (width - c * slot) % width, 1)
                other = jnp.where(nb < 0, before, jnp.where(nb >= bricks, after, other))
            here = jnp.where(own0, own, other) * gain0
            there = jnp.where(own1, own, other) * gain1
            parts.append((here + pltpu.roll(there, 1, 1)).astype(BF))
        field = jnp.concatenate(parts, axis=1)
        dot = functools.partial(jnp.dot, preferred_element_type=F32)
        half = 2 * plane
        mixed = dot(self.plane[:half], field) + dot(self.plane[half:], field)
        turn = jnp.where(s < 0, s + width, s)
        line = jnp.concatenate([self.line[k, pl.ds(turn, width), :] for k in range(2)], axis=0)
        line_high = line.astype(BF)
        line_low = (line - line_high.astype(F32)).astype(BF)
        lines = jnp.concatenate([line_high, line_low], axis=1)
        added = []
        for c in range(channels):
            wide = jnp.concatenate(
                [mixed[k * plane : (k + 1) * plane, c * width : (c + 1) * width] for k in range(2)],
                axis=1,
            )
            both = dot(wide.astype(BF), lines)
            result = (both[:, :width] + both[:, width:]).astype(BF)
            put(c, result)
            size = jnp.abs(result.astype(F32)).reshape(plane // 8, 8, width)
            added.append(totals[c] + jnp.sum(size, axis=0) * own_valid)
        return added


def no_totals(channels, width):
    return [jnp.zeros((8, width), F32) for _ in range(channels)]


def put_in(ref, n):
    def put(c, value):
        ref[n, c] = value

    return put


def load_kernel(picks, shift_ref, frac_ref, valid_ref, img_ref, plane_ref, line_ref, *refs):
    *part_refs, stat_ref, img_out, plane_out, line_out, brick_sem, table_sem = refs
    bricks, channels, _, width = img_ref.shape
    rank = lax.axis_index("round")
    copies = {}

    def fetch(b):
        return pltpu.make_async_copy(img_ref.at[b], img_out.at[b], brick_sem.at[b])

    tables = [
        pltpu.make_async_copy(plane_ref, plane_out, table_sem.at[0]),
        pltpu.make_async_copy(line_ref, line_out, table_sem.at[1]),
    ]
    if picks:
        base = picks[0](rank) - 1
    else:
        base = 0
    order = [lax.rem(base + n, bricks) for n in range(bricks)]
    for n, b in enumerate(order):
        copies[n] = fetch(b)
        copies[n].start()
        if n == 2:
            for table in tables:
                table.start()
    waited = 0
    totals = no_totals(channels, width)
    if picks:
        for waited in range(3):
            copies[waited].wait()
        for table in tables:
            table.wait()
        one = Filter(shift_ref, frac_ref, valid_ref, img_out, plane_out, line_out)
        totals = one(picks[0](rank), put_in(part_refs[0], 0), totals)
        waited = 3
    for n in range(waited, bricks):
        copies[n].wait()
    if picks:
        for k, pick in enumerate(picks[1:]):
            totals = one(pick(rank), put_in(part_refs[k + 1], 0), totals)
    else:
        for table in tables:
            table.wait()
    for c in range(channels):
        stat_ref[c] = totals[c]


def filter_kernel(groups, edge, last, shift_ref, frac_ref, valid_ref, img_ref, plane_ref, line_ref, sums_ref, *refs):
    halo = None
    if edge:
        halo, refs = refs[:2], refs[2:]
    *out_refs, stat_ref = refs
    _, channels, _, width = img_ref.shape
    rank = lax.axis_index("round")
    inner = Filter(shift_ref, frac_ref, valid_ref, img_ref, plane_ref, line_ref)
    outer = Filter(shift_ref, frac_ref, valid_ref, img_ref, plane_ref, line_ref, halo)
    totals = [sums_ref[c] for c in range(channels)]
    for picks, out_ref in zip(groups, out_refs, strict=True):
        for n, (pick, on_edge) in enumerate(picks):
            one = outer if on_edge else inner
            totals = one(pick(rank), put_in(out_ref, n), totals)
    if last:
        row = lax.broadcasted_iota(jnp.int32, (8, width), 0)
        packed = jnp.zeros((8, width), F32)
        for c in range(channels):
            packed = jnp.where(row == c, jnp.sum(totals[c]), packed)
        stat_ref[...] = packed
    else:
        for c in range(channels):
            stat_ref[c] = totals[c]


def norm_kernel(rounds, places, *refs):
    valid_ref, own_ref = refs[:2]
    stat_refs = refs[2 : 2 + rounds]
    *chunk_refs, out_ref, buf_ref, sem = refs[2 + rounds :]
    quota, channels, plane, width = own_ref.shape
    rank = lax.axis_index("round")
    count = jnp.maximum(jnp.sum(valid_ref[...]).astype(F32), 1.0)
    inverse = []
    for d in range(rounds):
        scale = stat_refs[d][...] / (count * (plane * width)) + 1e-06
        inverse.append(1.0 / scale)
    copies = []
    for j in range(quota):
        pos = jnp.where(rank == 0, quota - 1 - j, j)
        energy = jnp.zeros((plane, width), F32)

        def ratio(d, c):
            if d == 0:
                data = own_ref[j, c]
            else:
                g, n = places[d, j]
                data = chunk_refs[g][n, c]
            return data.astype(F32) * inverse[d][c : c + 1, :]

        for d in range(rounds):
            for c in range(channels):
                part = ratio(d, c)
                energy = energy + part * part
        factor = lax.rsqrt(energy * (1.0 / (rounds * channels)) + 1.0)
        for d in range(rounds):
            slot = lax.rem(rank + rounds - d, rounds)
            for c in range(channels):
                buf_ref[j, d, c] = (ratio(d, c) * factor).astype(BF)
            copy = pltpu.make_async_copy(buf_ref.at[j, d], out_ref.at[slot, 0, pos], sem.at[j, d])
            copy.start()
            copies.append(copy)
    for copy in copies:
        copy.wait()


def in_vmem(x):
    return pltpu.with_memory_space_constraint(x, pltpu.VMEM)


def in_hbm(x):
    return pltpu.with_memory_space_constraint(x, pltpu.HBM)


def body(image, shifts, fractions, valid):
    _, bricks, channels, depth, height, width = image.shape
    plane = depth * height
    rounds = lax.axis_size("round")
    count = lax.axis_size("brick")
    quota = bricks // rounds
    img = image.reshape(bricks, channels, plane, width)
    plane_table = jnp.asarray(plane_tables(depth, height))
    line_table = jnp.asarray(line_tables(width))

    def out(shape, dtype):
        return pltpu.VMEM(shape, dtype)

    def pick_for(d, j):
        def pick(rank):
            target = lax.rem(rank + d, rounds)
            return target * quota + jnp.where(target == 0, quota - 1 - j, j)

        return pick

    peers = range(1, rounds)
    early = [0] if quota > 1 else []
    inner = list(range(1, quota - 1))
    scalars = [shifts, fractions, valid]
    sum_shape = out((channels, 8, width), F32)

    *parts, sums, img_v, plane_v, line_v = pl.pallas_call(
        functools.partial(load_kernel, [pick_for(d, 0) for d in peers] if early else []),
        in_specs=[SMEM] * 3 + [HBM] * 3,
        out_specs=[VMEM] * ((rounds - 1) * len(early) + 4),
        out_shape=[out((1, channels, plane, width), BF)] * ((rounds - 1) * len(early))
        + [sum_shape, out(img.shape, BF), out(plane_table.shape, BF), out(line_table.shape, F32)],
        scratch_shapes=[pltpu.SemaphoreType.DMA((bricks,)), pltpu.SemaphoreType.DMA((2,))],
        name="load",
        compiler_params=PARAMS,
    )(*[in_hbm(a) for a in (*scalars, img, plane_table, line_table)])

    places = {}
    chunks = []

    def send(parts, js):
        for d, part in zip(peers, parts, strict=True):
            for n, j in enumerate(js):
                places[d, j] = len(chunks), n
            chunks.append(lax.ppermute(part, "round", [(i, (i + d) % rounds) for i in range(rounds)]))

    if early:
        send(parts, early)

    tail, head = pl.pallas_call(
        pack_kernel,
        in_specs=[SMEM, VMEM],
        out_specs=[VMEM, VMEM],
        out_shape=[out((plane, width), BF)] * 2,
        name="pack",
        compiler_params=PARAMS,
    )(valid, in_vmem(img_v))
    ends = count - 1
    before = lax.ppermute(tail, "brick", [(i, i + 1) for i in range(ends)])
    after = lax.ppermute(head, "brick", [(i + 1, i) for i in range(ends)])

    def filtered(groups, edge, last, sums):
        halo = [in_vmem(before), in_vmem(after)] if edge else []
        ins = [in_vmem(a) for a in (img_v, plane_v, line_v, sums)] + halo
        *parts, stat = pl.pallas_call(
            functools.partial(filter_kernel, groups, edge, last),
            in_specs=[SMEM] * 3 + [VMEM] * len(ins),
            out_specs=[VMEM] * (len(groups) + 1),
            out_shape=[out((len(g), channels, plane, width), BF) for g in groups]
            + [out((8, width), F32) if last else sum_shape],
            compiler_params=PARAMS,
        )(*scalars, *ins)
        return parts, stat

    if inner:
        parts, sums = filtered([[(pick_for(d, j), False) for j in inner] for d in peers], False, False, sums)
        send(parts, inner)
    edges = [quota - 1]
    groups = [[(pick_for(d, j), True) for j in edges] for d in peers]
    groups.append([(pick_for(0, j), j == quota - 1) for j in range(quota)])
    (*parts, own), stat = filtered(groups, True, True, sums)
    send(parts, edges)

    step = 1
    while step < count:
        stat = stat + lax.ppermute(stat, "brick", [(i, i ^ step) for i in range(count)])
        step *= 2
    stats = [stat]
    for d in peers:
        stats.append(lax.ppermute(stat, "round", [(i, (i + d) % rounds) for i in range(rounds)]))

    result = pl.pallas_call(
        functools.partial(norm_kernel, rounds, places),
        in_specs=[VMEM] * (2 + rounds + len(chunks)),
        out_specs=HBM,
        out_shape=jax.ShapeDtypeStruct((rounds, 1, quota, channels, plane, width), BF),
        scratch_shapes=[
            pltpu.VMEM((quota, rounds, channels, plane, width), BF),
            pltpu.SemaphoreType.DMA((quota, rounds)),
        ],
        name="norm",
        compiler_params=PARAMS,
    )(valid.reshape(1, -1), *[in_vmem(a) for a in (own, *stats, *chunks)])
    return result.reshape(rounds, 1, quota, channels, depth, height, width)


def solution(mesh):
    in_specs = (
        P("round", "brick", None, None, None, None),
        P("round", "brick"),
        P("round", "brick"),
        P(),
    )
    out_specs = P(None, "round", "brick", None, None, None, None)
    return jax.shard_map(body, mesh=mesh, in_specs=in_specs, out_specs=out_specs, check_vma=False)
```

```python
import functools

import jax
import jax.numpy as jnp
import numpy as np
from jax import lax
from jax.experimental import pallas as pl
from jax.experimental.pallas import tpu as pltpu
from jax.sharding import PartitionSpec as P

sigma_spot = 1.5


BF = jnp.bfloat16
F32 = jnp.float32
VMEM = pl.BlockSpec(memory_space=pltpu.VMEM)
SMEM = pl.BlockSpec(memory_space=pltpu.SMEM)
HBM = pl.BlockSpec(memory_space=pltpu.HBM)
CHUNKS = 4
HALVES = 2
PARAMS = pltpu.CompilerParams(vmem_limit_bytes=24 * 2**20)


def kernel_tables(count):
    index = np.arange(count, dtype=np.float64)
    offset = index[:, None] - index[None, :]
    smooth = np.exp(-offset * offset / (2.0 * sigma_spot * sigma_spot)) / (
        2.5066282746310002 * sigma_spot
    )
    smooth = np.where(np.abs(offset) < 4.0 * sigma_spot, smooth, 0.0)
    curve = (offset * offset / sigma_spot**4 - 1.0 / sigma_spot**2) * smooth
    return smooth, curve


def plane_tables(depth, height):
    gauss_z, curve_z = kernel_tables(depth)
    gauss_y, curve_y = kernel_tables(height)
    factor = -(sigma_spot * sigma_spot)
    with_bent = np.kron(gauss_z, gauss_y)
    with_smooth = np.kron(gauss_z, curve_y) + np.kron(curve_z, gauss_y)
    table = (factor * np.concatenate([with_bent, with_smooth], axis=0)).astype(np.float32)
    high = table.astype(BF)
    low = (table - high.astype(np.float32)).astype(BF)
    return np.concatenate([high, low], axis=0)


def line_tables(width):
    gauss_x, curve_x = kernel_tables(width)
    return np.stack([np.tile(t.T, (2, 1)) for t in (curve_x, gauss_x)]).astype(np.float32)


def lanes_of(shape):
    return lax.broadcasted_iota(jnp.int32, shape, len(shape) - 1)


def pack(valid_ref, img_ref, is_tail):
    bricks, channels, plane, width = img_ref.shape
    slot = width // channels
    first = lax.axis_index("brick") * bricks
    lane = lanes_of((plane, width))
    brick = jnp.where(is_tail, bricks - 1, 0)
    at = jnp.where(is_tail, width - slot, 0)
    row = jnp.zeros((plane, width), F32)
    for c in range(channels):
        data = img_ref[brick, c].astype(F32)
        moved = pltpu.roll(data, lax.rem(c * slot + width - at, width), 1)
        row = jnp.where(lane // slot == c, moved, row)
    return (row * valid_ref[first + brick].astype(F32)).astype(BF)


def swaps_of(count):
    both = lambda couples: [link for a, b in couples for link in ((a, b), (b, a))]
    even = both([(i, i + 1) for i in range(0, count - 1, 2)])
    if count % 4 or count < 8:
        return [even, both([(i, i + 1) for i in range(1, count - 1, 2)])]
    second = both([(i + 1, i + 2) for i in range(0, count, 4)] + [(i, i + 3) for i in range(0, count, 4)])
    third = both([(i, i + 1) for i in range(3, count - 1, 4)] + [(i, i + 1) for i in range(5, count - 4, 4)])
    for a, b, c in ((0, 1, 2), (count - 3, count - 2, count - 1)):
        third += [(a, b), (b, c), (c, a)]
    return [even, second, third]


class Filter:
    def __init__(self, shift_ref, frac_ref, valid_ref, img_ref, plane_ref=None, line_ref=None, halo=()):
        self.shift, self.frac, self.valid = shift_ref, frac_ref, valid_ref
        self.img, self.plane, self.line, self.halo = img_ref, plane_ref, line_ref, halo

    def valid_of(self, b):
        return self.valid[lax.axis_index("brick") * self.shift.shape[1] + b].astype(F32)

    def field(self, b, at, turned):
        bricks = self.shift.shape[1]
        _, channels, plane, width = self.img.shape
        slot = width // channels
        tiles = (plane // 8, 8, width)
        lane = lanes_of((8, width))
        s = self.shift[0, b]
        f = self.frac[0, b]
        right = s >= 0
        nb = jnp.where(right, b - 1, b + 1)
        nb_in = jnp.clip(nb, 0, bricks - 1)
        first = lax.axis_index("brick") * bricks
        own_valid = self.valid_of(b)
        nb_valid = self.valid_of(nb_in)
        if self.halo:
            there_is = jnp.logical_and(first + nb >= 0, first + nb < self.valid.shape[0])
            nb_valid = jnp.where(nb == nb_in, nb_valid, there_is.astype(F32))
            index = lax.axis_index("brick")
            in_first = (nb < 0) == (lax.rem(index, 2) == 1)
            second, third = self.halo[1], self.halo[-1]
            in_second = lax.rem(index, 4) % 3 != 0
            halo = jnp.where(in_second, second[...], third[...])
            halo = jnp.where(in_first, self.halo[0][...], halo).astype(F32).reshape(tiles)
            start = jnp.where(nb < 0, width - slot, 0)
        low0, high0 = jnp.where(right, 0, -s), jnp.where(right, width - s, width)
        low1, high1 = jnp.where(right, 0, -s - 1), jnp.where(right, width - s - 1, width)
        own0 = (lane >= low0) & (lane < high0)
        own1 = (lane >= low1) & (lane < high1)
        gain0 = (1.0 - f) * jnp.where(own0, own_valid, nb_valid)
        gain1 = f * jnp.where(own1, own_valid, nb_valid)
        own0, own1 = (jnp.broadcast_to(m, tiles) for m in (own0, own1))
        parts = []
        for c in range(channels):
            own = self.img[at(b), c].astype(F32).reshape(tiles)
            other = self.img[at(nb_in), c].astype(F32).reshape(tiles)
            if self.halo:
                moved = pltpu.roll(halo, lax.rem(start + (width - c * slot), width), 2)
                other = jnp.where(nb == nb_in, other, moved)
            here = jnp.where(own0, own, other) * gain0
            there = jnp.where(own1, own, other) * gain1
            value = here + pltpu.roll(there, 1, 2)
            if turned:
                value = pltpu.roll(value, self.turn_of(b), 2)
            parts.append(value.reshape(plane, width).astype(BF))
        return parts

    def turn_of(self, b):
        s = self.shift[0, b]
        return jnp.where(s < 0, s + self.img.shape[-1], s)

    def apply(self, parts, turn, put, totals, weight):
        plane, width = parts[0].shape
        field = jnp.concatenate(parts, axis=1)
        dot = functools.partial(jnp.dot, preferred_element_type=F32)
        half = 2 * plane
        mixed = dot(self.plane[:half], field) + dot(self.plane[half:], field)
        line = jnp.concatenate([self.line[k, pl.ds(turn, width), :] for k in range(2)], axis=0)
        line_high = line.astype(BF)
        line_low = (line - line_high.astype(F32)).astype(BF)
        lines = jnp.concatenate([line_high, line_low], axis=1)
        added = []
        for c, total in enumerate(totals):
            wide = jnp.concatenate(
                [mixed[k * plane : (k + 1) * plane, c * width : (c + 1) * width] for k in range(2)],
                axis=1,
            )
            both = dot(wide.astype(BF), lines)
            result = (both[:, :width] + both[:, width:]).astype(BF)
            put(c, result)
            size = jnp.abs(result.astype(F32)).reshape(plane // 8, 8, width)
            added.append(total + jnp.sum(size, axis=0) * weight)
        return added

    def __call__(self, b, put, totals):
        parts = self.field(b, lambda n: n, False)
        return self.apply(parts, self.turn_of(b), put, totals, self.valid_of(b))


def put_in(refs, n):
    def put(c, value):
        rows = value.shape[0] // len(refs)
        for k, ref in enumerate(refs):
            ref[n, c] = value[k * rows : (k + 1) * rows]

    return put


def load_kernel(picks, shift_hbm, frac_hbm, valid_hbm, img_ref, *refs):
    part_refs, refs = refs[: len(picks)], refs[len(picks) :]
    shift_ref, frac_ref, valid_ref, near_ref, near_sem, small_sem = refs
    bricks = img_ref.shape[0]
    rank = lax.axis_index("round")
    pairs = [(shift_hbm, shift_ref), (frac_hbm, frac_ref), (valid_hbm, valid_ref)]
    copies = [pltpu.make_async_copy(a, b, small_sem.at[n]) for n, (a, b) in enumerate(pairs)]
    bases = [pick(rank) - 1 for pick in picks]
    for k, base in enumerate(bases):
        for n in range(3):
            b = jnp.clip(base + n, 0, bricks - 1)
            copies.append(pltpu.make_async_copy(img_ref.at[b], near_ref.at[3 * k + n], near_sem.at[3 * k + n]))
    for copy in copies:
        copy.start()
    for copy in copies:
        copy.wait()
    one = Filter(shift_ref, frac_ref, valid_ref, near_ref)
    for k, (base, part_ref) in enumerate(zip(bases, part_refs, strict=True)):
        parts = one.field(base + 1, lambda n, k=k, base=base: n - base + 3 * k, True)
        for c, part in enumerate(parts):
            part_ref[0, c] = part


def pack_kernel(valid_ref, img_ref, swap0_ref, swap1_ref):
    even = lax.rem(lax.axis_index("brick"), 2) == 0
    swap0_ref[...] = pack(valid_ref, img_ref, even)
    swap1_ref[...] = pack(valid_ref, img_ref, jnp.logical_not(even))


def filter_kernel(groups, first, edge, shift_ref, frac_ref, valid_ref, img_ref, plane_ref, line_ref, *refs):
    sums_ref = None
    halo, refs = refs[:edge], refs[edge:]
    if not first:
        sums_ref, refs = refs[0], refs[1:]
    *out_refs, stat_ref = refs
    _, channels, _, width = img_ref.shape
    rank = lax.axis_index("round")
    one = Filter(shift_ref, frac_ref, valid_ref, img_ref, plane_ref, line_ref, halo)
    totals = [jnp.zeros((8, width), F32) if first else sums_ref[c] for c in range(channels)]
    for picks, halves in groups:
        refs, out_refs = out_refs[:halves], out_refs[halves:]
        for n, pick in enumerate(picks):
            totals = one(pick(rank), put_in(refs, n), totals)
    for c in range(channels):
        stat_ref[c] = totals[c]


def close_kernel(pick, shift_ref, frac_ref, valid_ref, plane_ref, line_ref, sums_ref, *refs):
    *refs, stat_ref = refs
    peers = len(refs) // 2
    part_refs, out_refs = refs[:peers], refs[peers:]
    channels, _, width = sums_ref.shape
    rank = lax.axis_index("round")
    one = Filter(shift_ref, frac_ref, valid_ref, None, plane_ref, line_ref)
    found = [sums_ref[c] for c in range(channels)]
    for part_ref, out_ref in zip(part_refs, out_refs, strict=True):
        parts = [part_ref[0, c] for c in range(channels)]
        totals = [jnp.zeros((8, width), F32) for _ in range(channels)]
        found += one.apply(parts, 0, put_in([out_ref], 0), totals, one.valid_of(pick(rank)))
    packed = jnp.zeros(stat_ref.shape[1:], F32)
    for n, total in enumerate(found):
        packed = jnp.where(lanes_of(packed.shape) == n, jnp.sum(total), packed)
    stat_ref[...] = jnp.broadcast_to(packed, stat_ref.shape)


def norm_kernel(rounds, tasks, out_ref, inverse_ref, data_refs, buf_refs, kept_ref, sem):
    _, channels, plane, width = out_ref.shape[2:]
    step = plane // CHUNKS
    tiles = (step // 8, 8, width)
    copies = []
    stored, kept = 0, 0
    for j, n, sources, keep in tasks:

        def ratio(d, c):
            g, m, base = sources[d]
            data = data_refs[g][m, c, n * step - base : (n + 1) * step - base]
            return data.astype(F32).reshape(tiles) * inverse_ref[d, c]

        energy = jnp.zeros(tiles, F32)
        for d in range(rounds):
            for c in range(channels):
                part = ratio(d, c)
                energy = energy + part * part
        factor = lax.rsqrt(energy * (1.0 / (rounds * channels)) + 1.0)
        to_ref, m = (kept_ref, kept) if keep else (buf_refs, stored)
        for d in range(rounds):
            for c in range(channels):
                to_ref[m, d, c] = (ratio(d, c) * factor).reshape(step, width).astype(BF)
        if keep:
            kept += 1
        else:
            copies += store(rounds, j, n, buf_refs.at[m], out_ref, sem.at[m])
            stored += 1
    return copies


def store(rounds, j, n, from_ref, out_ref, sem):
    quota, _, plane, _ = out_ref.shape[2:]
    rank = lax.axis_index("round")
    pos = jnp.where(rank == 0, quota - 1 - j, j)
    step = plane // CHUNKS
    copies = []
    for d in range(rounds):
        slot = lax.rem(rank + rounds - d, rounds)
        to_ref = out_ref.at[slot, 0, pos, :, pl.ds(n * step, step)]
        copy = pltpu.make_async_copy(from_ref.at[d], to_ref, sem.at[d])
        copy.start()
        copies.append(copy)
    return copies


def norm1_kernel(rounds, shared, tasks, valid_ref, stat_ref, *refs):
    *data_refs, out_ref, inverse_ref, kept_ref, buf_ref, sem = refs
    _, channels, plane, width = out_ref.shape[2:]
    rank = lax.axis_index("round")
    count = jnp.maximum(jnp.sum(valid_ref[...]).astype(F32), 1.0)
    each = stat_ref.shape[0] // rounds
    for d in range(rounds):
        slot = lax.rem(rank + rounds - d, rounds)
        total = jnp.zeros(stat_ref.shape[1:], F32)
        for e in range(rounds if shared else 1):
            part = jnp.sum(stat_ref[pl.ds(lax.rem(slot + e, rounds) * each, each)], axis=0)
            total = total + (pltpu.roll(part, width - e * channels, 1) if e else part)
        scale = total / (count * (plane * width)) + 1e-06
        for c in range(channels):
            inverse_ref[d, c] = jnp.broadcast_to((1.0 / scale)[:, c : c + 1], (8, width))
    for copy in norm_kernel(rounds, tasks, out_ref, inverse_ref, data_refs, buf_ref, kept_ref, sem):
        copy.wait()


def norm2_kernel(rounds, tasks, carried, result_ref, inverse_ref, kept_ref, *refs):
    *data_refs, out_ref, buf_ref, sem, kept_sem = refs
    copies = []
    for m, (j, n) in enumerate(carried):
        copies += store(rounds, j, n, kept_ref.at[m], out_ref, kept_sem.at[m])
    copies += norm_kernel(rounds, tasks, out_ref, inverse_ref, data_refs, buf_ref, None, sem)
    for copy in copies:
        copy.wait()


def in_vmem(x):
    return pltpu.with_memory_space_constraint(x, pltpu.VMEM)


def in_smem(x):
    return pltpu.with_memory_space_constraint(x, pltpu.SMEM)


def in_hbm(x):
    return pltpu.with_memory_space_constraint(x, pltpu.HBM)


def body(image, shifts, fractions, valid):
    _, bricks, channels, depth, height, width = image.shape
    plane = depth * height
    rounds = lax.axis_size("round")
    count = lax.axis_size("brick")
    quota = bricks // rounds
    img = image.reshape(bricks, channels, plane, width)
    plane_table = jnp.asarray(plane_tables(depth, height))
    line_table = jnp.asarray(line_tables(width))

    def out(shape, dtype):
        return pltpu.VMEM(shape, dtype)

    def pick_for(d, j):
        def pick(rank):
            target = lax.rem(rank + d, rounds)
            return target * quota + jnp.where(target == 0, quota - 1 - j, j)

        return pick

    peers = range(1, rounds)
    early = [0] if quota > 1 else []
    inner = list(range(1, quota - 1))
    sum_shape = out((channels, 8, width), F32)
    firsts = [pick_for(d, 0) for d in peers] if early else []
    sources = [shifts, fractions, valid]

    *parts, shift_s, frac_s, valid_s = pl.pallas_call(
        functools.partial(load_kernel, firsts),
        in_specs=[HBM] * 4,
        out_specs=[VMEM] * len(firsts) + [SMEM] * 3,
        out_shape=[out((1, channels, plane, width), BF)] * len(firsts)
        + [pltpu.SMEM(a.shape, a.dtype) for a in sources],
        scratch_shapes=[
            pltpu.VMEM((3 * max(len(firsts), 1), channels, plane, width), BF),
            pltpu.SemaphoreType.DMA((3 * max(len(firsts), 1),)),
            pltpu.SemaphoreType.DMA((3,)),
        ],
        name="load",
        compiler_params=PARAMS,
    )(*[in_hbm(a) for a in (*sources, img)])
    scalars = [in_smem(a) for a in (shift_s, frac_s, valid_s)]
    tables = [in_vmem(a) for a in (plane_table, line_table)]

    def send(parts):
        chunks = []
        for d, part in zip(peers, parts, strict=True):
            chunks.append(lax.ppermute(part, "round", [(i, (i + d) % rounds) for i in range(rounds)]))
        return chunks

    def filtered(groups, sums, halo=()):
        ins = [in_vmem(img), *tables, *[in_vmem(a) for a in (*halo, *sums)]]
        return pl.pallas_call(
            functools.partial(filter_kernel, groups, not sums, len(halo)),
            in_specs=[SMEM] * 3 + [VMEM] * len(ins),
            out_specs=[VMEM] * (sum(halves for _, halves in groups) + 1),
            out_shape=[
                out((len(g), channels, plane // halves, width), BF) for g, halves in groups for _ in range(halves)
            ]
            + [sum_shape],
            compiler_params=PARAMS,
        )(*scalars, *ins)

    shifted = send(parts) if early else []
    swaps = pl.pallas_call(
        pack_kernel,
        in_specs=[SMEM, VMEM],
        out_specs=[VMEM] * 2,
        out_shape=[out((plane, width), BF)] * 2,
        name="pack",
        compiler_params=PARAMS,
    )(scalars[2], in_vmem(img))
    halo = []
    for links, swap in zip(swaps_of(count), (swaps[0], swaps[1], swaps[1])):
        halo.append(lax.ppermute(swap, "brick", links))
    sums = []
    if inner:
        *parts, stat = filtered([([pick_for(d, j) for j in inner], 1) for d in peers], sums)
        sums = [stat]
        arrived_inner = send(parts)
    last = quota - 1
    if last:
        own, stat = filtered([([pick_for(0, j) for j in range(last)], 1)], sums)
        sums = [stat]
    groups = [([pick_for(0, last)], 1)] + [([pick_for(d, last)], HALVES) for d in peers]
    own_last, *parts, stat = filtered(groups, sums, halo)
    ins = [*tables, *[in_vmem(a) for a in (stat, *shifted)]]
    *arrived, stat = pl.pallas_call(
        functools.partial(close_kernel, pick_for(0, 0)),
        in_specs=[SMEM] * 3 + [VMEM] * len(ins),
        out_specs=[VMEM] * (len(shifted) + 1),
        out_shape=[out((1, channels, plane, width), BF)] * len(shifted)
        + [jax.ShapeDtypeStruct((rounds * count, 1, width), F32)],
        name="k4",
        compiler_params=PARAMS,
    )(*scalars, *ins)
    stats = lax.all_to_all(stat, ("round", "brick"), split_axis=0, concat_axis=0, tiled=True)

    arrived_last = [send(parts[k::HALVES]) for k in range(HALVES)]

    part = plane // HALVES
    step = plane // CHUNKS

    def task(j, n, keep, arrays):
        if j < last:
            theirs = arrived if j == 0 else arrived_inner
            found = [(own, j, 0)] + [(a, 0 if j == 0 else j - 1, 0) for a in theirs]
        else:
            k = n * step // part
            found = [(own_last, 0, 0)] + [(a, 0, k * part) for a in arrived_last[k]]
        sources = []
        for array, m, base in found:
            if all(array is not a for a in arrays):
                arrays.append(array)
            sources.append(([array is a for a in arrays].index(True), m, base))
        return j, n, sources, keep

    pieces = [(j, n) for j in range(quota) for n in range(CHUNKS)]
    late = pieces[len(pieces) - CHUNKS // HALVES :]
    pieces = pieces[: len(pieces) - len(late)]
    carried = pieces[len(pieces) * 4 // 7 :]
    arrays = []
    tasks = [task(j, n, (j, n) in carried, arrays) for j, n in pieces]
    tile = (rounds, channels, step, width)
    ins = [in_vmem(a) for a in (valid.reshape(1, -1), stats, *arrays)]
    stored = max(len(pieces) - len(carried), 1)
    result, inverse, kept = pl.pallas_call(
        functools.partial(norm1_kernel, rounds, bool(early), tasks),
        in_specs=[VMEM] * len(ins),
        out_specs=[HBM, VMEM, VMEM],
        out_shape=[
            jax.ShapeDtypeStruct((rounds, 1, quota, channels, plane, width), BF),
            out((rounds, channels, 8, width), F32),
            out((len(carried), *tile), BF),
        ],
        scratch_shapes=[pltpu.VMEM((stored, *tile), BF), pltpu.SemaphoreType.DMA((stored, rounds))],
        name="norm1",
        compiler_params=PARAMS,
    )(*ins)
    arrays = []
    tasks = [task(j, n, False, arrays) for j, n in late]
    ins = [in_hbm(result)] + [in_vmem(a) for a in (inverse, kept, *arrays)]
    result = pl.pallas_call(
        functools.partial(norm2_kernel, rounds, tasks, carried),
        in_specs=[HBM] + [VMEM] * (len(ins) - 1),
        out_specs=HBM,
        out_shape=jax.ShapeDtypeStruct(result.shape, BF),
        scratch_shapes=[
            pltpu.VMEM((len(late), *tile), BF),
            pltpu.SemaphoreType.DMA((len(late), rounds)),
            pltpu.SemaphoreType.DMA((len(carried), rounds)),
        ],
        input_output_aliases={0: 0},
        name="norm2",
        compiler_params=PARAMS,
    )(*ins)
    return result.reshape(rounds, 1, quota, channels, depth, height, width)


def solution(mesh):
    in_specs = (
        P("round", "brick", None, None, None, None),
        P("round", "brick"),
        P("round", "brick"),
        P(),
    )
    out_specs = P(None, "round", "brick", None, None, None, None)
    return jax.shard_map(body, mesh=mesh, in_specs=in_specs, out_specs=out_specs, check_vma=False)
```

```python
import functools

import jax
import jax.numpy as jnp
import numpy as np
from jax import lax
from jax.experimental import pallas as pl
from jax.experimental.pallas import tpu as pltpu
from jax.sharding import PartitionSpec as P

sigma_spot = 1.5


BF = jnp.bfloat16
F32 = jnp.float32
VMEM = pl.BlockSpec(memory_space=pltpu.VMEM)
SMEM = pl.BlockSpec(memory_space=pltpu.SMEM)
HBM = pl.BlockSpec(memory_space=pltpu.HBM)
CHUNKS = 4
HALVES = 2
ROWS = 16
PARAMS = pltpu.CompilerParams(vmem_limit_bytes=24 * 2**20)


def kernel_tables(count):
    index = np.arange(count, dtype=np.float64)
    offset = index[:, None] - index[None, :]
    smooth = np.exp(-offset * offset / (2.0 * sigma_spot * sigma_spot)) / (
        2.5066282746310002 * sigma_spot
    )
    smooth = np.where(np.abs(offset) < 4.0 * sigma_spot, smooth, 0.0)
    curve = (offset * offset / sigma_spot**4 - 1.0 / sigma_spot**2) * smooth
    return smooth, curve


def plane_tables(depth, height):
    gauss_z, curve_z = kernel_tables(depth)
    gauss_y, curve_y = kernel_tables(height)
    factor = -(sigma_spot * sigma_spot)
    with_bent = np.kron(gauss_z, gauss_y)
    with_smooth = np.kron(gauss_z, curve_y) + np.kron(curve_z, gauss_y)
    table = (factor * np.concatenate([with_bent, with_smooth], axis=0)).astype(np.float32)
    high = table.astype(BF)
    low = (table - high.astype(np.float32)).astype(BF)
    return np.concatenate([high, low], axis=0)


def line_tables(width):
    gauss_x, curve_x = kernel_tables(width)
    return np.stack([np.tile(t.T, (2, 1)) for t in (curve_x, gauss_x)]).astype(np.float32)


def lanes_of(shape):
    return lax.broadcasted_iota(jnp.int32, shape, len(shape) - 1)


def pack(valid_ref, img_ref, is_tail):
    bricks, channels, plane, width = img_ref.shape
    slot = width // channels
    first = lax.axis_index("brick") * bricks
    lane = lanes_of((plane, width))
    brick = jnp.where(is_tail, bricks - 1, 0)
    at = jnp.where(is_tail, width - slot, 0)
    row = jnp.zeros((plane, width), F32)
    for c in range(channels):
        data = img_ref[brick, c].astype(F32)
        moved = pltpu.roll(data, lax.rem(c * slot + width - at, width), 1)
        row = jnp.where(lane // slot == c, moved, row)
    return (row * valid_ref[first + brick].astype(F32)).astype(BF)


def swaps_of(count):
    both = lambda couples: [link for a, b in couples for link in ((a, b), (b, a))]
    even = both([(i, i + 1) for i in range(0, count - 1, 2)])
    if count % 4 or count < 8:
        return [even, both([(i, i + 1) for i in range(1, count - 1, 2)])]
    second = both([(i + 1, i + 2) for i in range(0, count, 4)] + [(i, i + 3) for i in range(0, count, 4)])
    third = both([(i, i + 1) for i in range(3, count - 1, 4)] + [(i, i + 1) for i in range(5, count - 4, 4)])
    for a, b, c in ((0, 1, 2), (count - 3, count - 2, count - 1)):
        third += [(a, b), (b, c), (c, a)]
    return [even, second, third]


class Filter:
    def __init__(self, shift_ref, frac_ref, valid_ref, img_ref, plane_ref=None, line_ref=None, halo=()):
        self.shift, self.frac, self.valid = shift_ref, frac_ref, valid_ref
        self.img, self.plane, self.line, self.halo = img_ref, plane_ref, line_ref, halo

    def valid_of(self, b):
        return self.valid[lax.axis_index("brick") * self.shift.shape[1] + b].astype(F32)

    def field(self, b, at, turned):
        bricks = self.shift.shape[1]
        _, channels, plane, width = self.img.shape
        slot = width // channels
        tiles = (plane // 8, 8, width)
        lane = lanes_of((8, width))
        s = self.shift[0, b]
        f = self.frac[0, b]
        right = s >= 0
        nb = jnp.where(right, b - 1, b + 1)
        nb_in = jnp.clip(nb, 0, bricks - 1)
        first = lax.axis_index("brick") * bricks
        own_valid = self.valid_of(b)
        nb_valid = self.valid_of(nb_in)
        if self.halo:
            there_is = jnp.logical_and(first + nb >= 0, first + nb < self.valid.shape[0])
            nb_valid = jnp.where(nb == nb_in, nb_valid, there_is.astype(F32))
            index = lax.axis_index("brick")
            in_first = (nb < 0) == (lax.rem(index, 2) == 1)
            second, third = self.halo[1], self.halo[-1]
            in_second = lax.rem(index, 4) % 3 != 0
            halo = jnp.where(in_second, second[...], third[...])
            halo = jnp.where(in_first, self.halo[0][...], halo).astype(F32).reshape(tiles)
            start = jnp.where(nb < 0, width - slot, 0)
        low0, high0 = jnp.where(right, 0, -s), jnp.where(right, width - s, width)
        low1, high1 = jnp.where(right, 0, -s - 1), jnp.where(right, width - s - 1, width)
        own0 = (lane >= low0) & (lane < high0)
        own1 = (lane >= low1) & (lane < high1)
        gain0 = (1.0 - f) * jnp.where(own0, own_valid, nb_valid)
        gain1 = f * jnp.where(own1, own_valid, nb_valid)
        own0, own1 = (jnp.broadcast_to(m, tiles) for m in (own0, own1))
        if turned:
            row = lax.broadcasted_iota(jnp.int32, (width, width), 0) + self.turn_of(b)
            row = jnp.where(row >= width, row - width, row)
            turn = (row == lanes_of((width, width))).astype(F32).astype(BF)
        parts = []
        for c in range(channels):
            own = self.img[at(b), c].astype(F32).reshape(tiles)
            other = self.img[at(nb_in), c].astype(F32).reshape(tiles)
            if self.halo:
                moved = pltpu.roll(halo, lax.rem(start + (width - c * slot), width), 2)
                other = jnp.where(nb == nb_in, other, moved)
            here = jnp.where(own0, own, other) * gain0
            there = jnp.where(own1, own, other) * gain1
            value = (here + pltpu.roll(there, 1, 2)).reshape(plane, width).astype(BF)
            if turned:
                value = jnp.dot(value, turn, preferred_element_type=F32).astype(BF)
            parts.append(value)
        return parts

    def turn_of(self, b):
        s = self.shift[0, b]
        return jnp.where(s < 0, s + self.img.shape[-1], s)

    def apply(self, parts, turn, put, totals, weight):
        plane, width = parts[0].shape
        field = jnp.concatenate(parts, axis=1)
        dot = functools.partial(jnp.dot, preferred_element_type=F32)
        half = 2 * plane
        mixed = dot(self.plane[:half], field) + dot(self.plane[half:], field)
        line = jnp.concatenate([self.line[k, pl.ds(turn, width), :] for k in range(2)], axis=0)
        line_high = line.astype(BF)
        line_low = (line - line_high.astype(F32)).astype(BF)
        lines = jnp.concatenate([line_high, line_low], axis=1)
        added = []
        for c, total in enumerate(totals):
            wide = jnp.concatenate(
                [mixed[k * plane : (k + 1) * plane, c * width : (c + 1) * width] for k in range(2)],
                axis=1,
            )
            both = dot(wide.astype(BF), lines)
            result = (both[:, :width] + both[:, width:]).astype(BF)
            put(c, result)
            size = jnp.abs(result.astype(F32)).reshape(plane // 8, 8, width)
            added.append(total + jnp.sum(size, axis=0) * weight)
        return added

    def __call__(self, b, put, totals):
        parts = self.field(b, lambda n: n, False)
        return self.apply(parts, self.turn_of(b), put, totals, self.valid_of(b))


def put_in(refs, n):
    def put(c, value):
        rows = value.shape[0] // len(refs)
        for k, ref in enumerate(refs):
            ref[n, c] = value[k * rows : (k + 1) * rows]

    return put


def load_kernel(picks, shift_hbm, frac_hbm, valid_hbm, img_ref, *refs):
    part_refs, refs = refs[: len(picks)], refs[len(picks) :]
    shift_ref, frac_ref, valid_ref, near_ref, near_sem, small_sem = refs
    bricks = img_ref.shape[0]
    rank = lax.axis_index("round")
    pairs = [(shift_hbm, shift_ref), (frac_hbm, frac_ref), (valid_hbm, valid_ref)]
    copies = [pltpu.make_async_copy(a, b, small_sem.at[n]) for n, (a, b) in enumerate(pairs)]
    bases = [pick(rank) - 1 for pick in picks]
    for k, base in enumerate(bases):
        for n in range(3):
            b = jnp.clip(base + n, 0, bricks - 1)
            copies.append(pltpu.make_async_copy(img_ref.at[b], near_ref.at[3 * k + n], near_sem.at[3 * k + n]))
    for copy in copies:
        copy.start()
    for copy in copies:
        copy.wait()
    one = Filter(shift_ref, frac_ref, valid_ref, near_ref)
    for k, (base, part_ref) in enumerate(zip(bases, part_refs, strict=True)):
        parts = one.field(base + 1, lambda n, k=k, base=base: n - base + 3 * k, True)
        for c, part in enumerate(parts):
            part_ref[0, c] = part


def pack_kernel(valid_ref, img_ref, swap0_ref, swap1_ref):
    even = lax.rem(lax.axis_index("brick"), 2) == 0
    swap0_ref[...] = pack(valid_ref, img_ref, even)
    swap1_ref[...] = pack(valid_ref, img_ref, jnp.logical_not(even))


def filter_kernel(groups, first, edge, ahead, behind, shift_ref, frac_ref, valid_ref, img_ref, plane_ref, line_ref, *refs):
    sums_ref = None
    halo, refs = refs[:edge], refs[edge:]
    if not first:
        sums_ref, refs = refs[0], refs[1:]
    if behind:
        field_ref, refs = refs[0], refs[1:]
    *out_refs, stat_ref = refs
    if ahead:
        *out_refs, next_ref = out_refs
    _, channels, _, width = img_ref.shape
    rank = lax.axis_index("round")
    one = Filter(shift_ref, frac_ref, valid_ref, img_ref, plane_ref, line_ref, halo)
    totals = [jnp.zeros((8, width), F32) if first else sums_ref[c] for c in range(channels)]
    for picks, halves in groups:
        refs, out_refs = out_refs[:halves], out_refs[halves:]
        for n, pick in enumerate(picks):
            b = pick(rank)
            if behind:
                parts = [field_ref[c] for c in range(channels)]
                totals = one.apply(parts, one.turn_of(b), put_in(refs, n), totals, one.valid_of(b))
            else:
                totals = one(b, put_in(refs, n), totals)
            behind = False
    if ahead:
        for c, part in enumerate(one.field(ahead(rank), lambda n: n, False)):
            next_ref[c] = part
    for c in range(channels):
        stat_ref[c] = totals[c]


def close_kernel(pick, shift_ref, frac_ref, valid_ref, plane_ref, line_ref, sums_ref, *refs):
    *refs, stat_ref = refs
    peers = len(refs) // 2
    part_refs, out_refs = refs[:peers], refs[peers:]
    channels, _, width = sums_ref.shape
    rank = lax.axis_index("round")
    one = Filter(shift_ref, frac_ref, valid_ref, None, plane_ref, line_ref)
    found = [sums_ref[c] for c in range(channels)]
    for part_ref, out_ref in zip(part_refs, out_refs, strict=True):
        parts = [part_ref[0, c] for c in range(channels)]
        totals = [jnp.zeros((8, width), F32) for _ in range(channels)]
        found += one.apply(parts, 0, put_in([out_ref], 0), totals, one.valid_of(pick(rank)))
    packed = jnp.zeros(stat_ref.shape[1:], F32)
    for n, total in enumerate(found):
        packed = jnp.where(lanes_of(packed.shape) == n, jnp.sum(total), packed)
    stat_ref[...] = jnp.broadcast_to(packed, stat_ref.shape)


def norm_kernel(rounds, tasks, out_ref, inverse_ref, data_refs, buf_refs, kept_ref, sem):
    _, channels, plane, width = out_ref.shape[2:]
    step = plane // CHUNKS
    tiles = (ROWS // 8, 8, width)
    copies = []
    stored, kept = 0, 0
    for j, n, sources, keep in tasks:
        to_ref, m = (kept_ref, kept) if keep else (buf_refs, stored)
        for first in range(0, step, ROWS):
            ratios = []
            energy = jnp.zeros(tiles, F32)
            for d in range(rounds):
                g, k, base = sources[d]
                begin = n * step - base + first
                for c in range(channels):
                    data = data_refs[g][k, c, begin : begin + ROWS]
                    ratio = data.astype(F32).reshape(tiles) * inverse_ref[d, c]
                    energy = energy + ratio * ratio
                    ratios.append(ratio)
            factor = lax.rsqrt(energy * (1.0 / (rounds * channels)) + 1.0)
            for d in range(rounds):
                for c in range(channels):
                    value = (ratios[d * channels + c] * factor).reshape(ROWS, width).astype(BF)
                    to_ref[m, d, c, first : first + ROWS] = value
        if keep:
            kept += 1
        else:
            copies += store(rounds, j, n, buf_refs.at[m], out_ref, sem.at[m])
            stored += 1
    return copies


def store(rounds, j, n, from_ref, out_ref, sem):
    quota, _, plane, _ = out_ref.shape[2:]
    rank = lax.axis_index("round")
    pos = jnp.where(rank == 0, quota - 1 - j, j)
    step = plane // CHUNKS
    copies = []
    for d in range(rounds):
        slot = lax.rem(rank + rounds - d, rounds)
        to_ref = out_ref.at[slot, 0, pos, :, pl.ds(n * step, step)]
        copy = pltpu.make_async_copy(from_ref.at[d], to_ref, sem.at[d])
        copy.start()
        copies.append(copy)
    return copies


def norm1_kernel(rounds, shared, tasks, valid_ref, stat_ref, *refs):
    *data_refs, out_ref, inverse_ref, kept_ref, buf_ref, sem = refs
    _, channels, plane, width = out_ref.shape[2:]
    rank = lax.axis_index("round")
    count = jnp.maximum(jnp.sum(valid_ref[...]).astype(F32), 1.0)
    each = stat_ref.shape[0] // rounds
    for d in range(rounds):
        slot = lax.rem(rank + rounds - d, rounds)
        total = jnp.zeros(stat_ref.shape[1:], F32)
        for e in range(rounds if shared else 1):
            part = jnp.sum(stat_ref[pl.ds(lax.rem(slot + e, rounds) * each, each)], axis=0)
            total = total + (pltpu.roll(part, width - e * channels, 1) if e else part)
        scale = total / (count * (plane * width)) + 1e-06
        for c in range(channels):
            inverse_ref[d, c] = jnp.broadcast_to((1.0 / scale)[:, c : c + 1], (8, width))
    for copy in norm_kernel(rounds, tasks, out_ref, inverse_ref, data_refs, buf_ref, kept_ref, sem):
        copy.wait()


def norm2_kernel(rounds, tasks, carried, result_ref, inverse_ref, kept_ref, *refs):
    *data_refs, out_ref, buf_ref, sem, kept_sem = refs
    copies = []
    for m, (j, n) in enumerate(carried):
        copies += store(rounds, j, n, kept_ref.at[m], out_ref, kept_sem.at[m])
    copies += norm_kernel(rounds, tasks, out_ref, inverse_ref, data_refs, buf_ref, None, sem)
    for copy in copies:
        copy.wait()


def in_vmem(x):
    return pltpu.with_memory_space_constraint(x, pltpu.VMEM)


def in_smem(x):
    return pltpu.with_memory_space_constraint(x, pltpu.SMEM)


def in_hbm(x):
    return pltpu.with_memory_space_constraint(x, pltpu.HBM)


def body(image, shifts, fractions, valid):
    _, bricks, channels, depth, height, width = image.shape
    plane = depth * height
    rounds = lax.axis_size("round")
    count = lax.axis_size("brick")
    quota = bricks // rounds
    img = image.reshape(bricks, channels, plane, width)
    plane_table = jnp.asarray(plane_tables(depth, height))
    line_table = jnp.asarray(line_tables(width))

    def out(shape, dtype):
        return pltpu.VMEM(shape, dtype)

    def pick_for(d, j):
        def pick(rank):
            target = lax.rem(rank + d, rounds)
            return target * quota + jnp.where(target == 0, quota - 1 - j, j)

        return pick

    peers = range(1, rounds)
    early = [0] if quota > 1 else []
    inner = list(range(1, quota - 1))
    sum_shape = out((channels, 8, width), F32)
    firsts = [pick_for(d, 0) for d in peers] if early else []
    sources = [shifts, fractions, valid]

    *parts, shift_s, frac_s, valid_s = pl.pallas_call(
        functools.partial(load_kernel, firsts),
        in_specs=[HBM] * 4,
        out_specs=[VMEM] * len(firsts) + [SMEM] * 3,
        out_shape=[out((1, channels, plane, width), BF)] * len(firsts)
        + [pltpu.SMEM(a.shape, a.dtype) for a in sources],
        scratch_shapes=[
            pltpu.VMEM((3 * max(len(firsts), 1), channels, plane, width), BF),
            pltpu.SemaphoreType.DMA((3 * max(len(firsts), 1),)),
            pltpu.SemaphoreType.DMA((3,)),
        ],
        name="load",
        compiler_params=PARAMS,
    )(*[in_hbm(a) for a in (*sources, img)])
    scalars = [in_smem(a) for a in (shift_s, frac_s, valid_s)]
    tables = [in_vmem(a) for a in (plane_table, line_table)]

    def send(parts):
        chunks = []
        for d, part in zip(peers, parts, strict=True):
            chunks.append(lax.ppermute(part, "round", [(i, (i + d) % rounds) for i in range(rounds)]))
        return chunks

    def filtered(groups, sums, halo=(), ahead=None, field=()):
        ins = [in_vmem(img), *tables, *[in_vmem(a) for a in (*halo, *sums, *field)]]
        return pl.pallas_call(
            functools.partial(filter_kernel, groups, not sums, len(halo), ahead, bool(field)),
            in_specs=[SMEM] * 3 + [VMEM] * len(ins),
            out_specs=[VMEM] * (sum(halves for _, halves in groups) + bool(ahead) + 1),
            out_shape=[
                out((len(g), channels, plane // halves, width), BF) for g, halves in groups for _ in range(halves)
            ]
            + [out(img.shape[1:], BF)] * bool(ahead)
            + [sum_shape],
            compiler_params=PARAMS,
        )(*scalars, *ins)

    shifted = send(parts) if early else []
    swaps = pl.pallas_call(
        pack_kernel,
        in_specs=[SMEM, VMEM],
        out_specs=[VMEM] * 2,
        out_shape=[out((plane, width), BF)] * 2,
        name="pack",
        compiler_params=PARAMS,
    )(scalars[2], in_vmem(img))
    halo = []
    for links, swap in zip(swaps_of(count), (swaps[0], swaps[1], swaps[1])):
        halo.append(lax.ppermute(swap, "brick", links))
    sums, fields = [], []
    if inner:
        groups = [([pick_for(d, j) for j in inner], 1) for d in peers]
        *parts, field, stat = filtered(groups, sums, ahead=pick_for(0, 0))
        fields = [field]
        sums = [stat]
        arrived_inner = send(parts)
    last = quota - 1
    if last:
        own, stat = filtered([([pick_for(0, j) for j in range(last)], 1)], sums, field=fields)
        sums = [stat]
    groups = [([pick_for(0, last)], 1)] + [([pick_for(d, last)], HALVES) for d in peers]
    own_last, *parts, stat = filtered(groups, sums, halo)
    ins = [*tables, *[in_vmem(a) for a in (stat, *shifted)]]
    *arrived, stat = pl.pallas_call(
        functools.partial(close_kernel, pick_for(0, 0)),
        in_specs=[SMEM] * 3 + [VMEM] * len(ins),
        out_specs=[VMEM] * (len(shifted) + 1),
        out_shape=[out((1, channels, plane, width), BF)] * len(shifted)
        + [jax.ShapeDtypeStruct((rounds * count, 1, width), F32)],
        name="k4",
        compiler_params=PARAMS,
    )(*scalars, *ins)
    stats = lax.all_to_all(stat, ("round", "brick"), split_axis=0, concat_axis=0, tiled=True)

    arrived_last = [send(parts[k::HALVES]) for k in range(HALVES)]

    part = plane // HALVES
    step = plane // CHUNKS

    def task(j, n, keep, arrays):
        if j < last:
            theirs = arrived if j == 0 else arrived_inner
            found = [(own, j, 0)] + [(a, 0 if j == 0 else j - 1, 0) for a in theirs]
        else:
            k = n * step // part
            found = [(own_last, 0, 0)] + [(a, 0, k * part) for a in arrived_last[k]]
        sources = []
        for array, m, base in found:
            if all(array is not a for a in arrays):
                arrays.append(array)
            sources.append(([array is a for a in arrays].index(True), m, base))
        return j, n, sources, keep

    pieces = [(j, n) for j in range(quota) for n in range(CHUNKS)]
    late = pieces[len(pieces) - CHUNKS // HALVES :]
    pieces = pieces[: len(pieces) - len(late)]
    carried = pieces[len(pieces) * 6 // 7 :]
    arrays = []
    tasks = [task(j, n, (j, n) in carried, arrays) for j, n in pieces]
    tile = (rounds, channels, step, width)
    ins = [in_vmem(a) for a in (valid.reshape(1, -1), stats, *arrays)]
    stored = max(len(pieces) - len(carried), 1)
    result, inverse, kept = pl.pallas_call(
        functools.partial(norm1_kernel, rounds, bool(early), tasks),
        in_specs=[VMEM] * len(ins),
        out_specs=[HBM, VMEM, VMEM],
        out_shape=[
            jax.ShapeDtypeStruct((rounds, 1, quota, channels, plane, width), BF),
            out((rounds, channels, 8, width), F32),
            out((len(carried), *tile), BF),
        ],
        scratch_shapes=[pltpu.VMEM((stored, *tile), BF), pltpu.SemaphoreType.DMA((stored, rounds))],
        name="norm1",
        compiler_params=PARAMS,
    )(*ins)
    arrays = []
    tasks = [task(j, n, False, arrays) for j, n in late]
    ins = [in_hbm(result)] + [in_vmem(a) for a in (inverse, kept, *arrays)]
    result = pl.pallas_call(
        functools.partial(norm2_kernel, rounds, tasks, carried),
        in_specs=[HBM] + [VMEM] * (len(ins) - 1),
        out_specs=HBM,
        out_shape=jax.ShapeDtypeStruct(result.shape, BF),
        scratch_shapes=[
            pltpu.VMEM((len(late), *tile), BF),
            pltpu.SemaphoreType.DMA((len(late), rounds)),
            pltpu.SemaphoreType.DMA((len(carried), rounds)),
        ],
        input_output_aliases={0: 0},
        name="norm2",
        compiler_params=PARAMS,
    )(*ins)
    return result.reshape(rounds, 1, quota, channels, depth, height, width)


def solution(mesh):
    in_specs = (
        P("round", "brick", None, None, None, None),
        P("round", "brick"),
        P("round", "brick"),
        P(),
    )
    out_specs = P(None, "round", "brick", None, None, None, None)
    return jax.shard_map(body, mesh=mesh, in_specs=in_specs, out_specs=out_specs, check_vma=False)
```

```python
import functools

import jax
import jax.numpy as jnp
import numpy as np
from jax import lax
from jax.experimental import pallas as pl
from jax.experimental.pallas import tpu as pltpu
from jax.sharding import PartitionSpec as P

sigma_spot = 1.5


BF = jnp.bfloat16
F32 = jnp.float32
VMEM = pl.BlockSpec(memory_space=pltpu.VMEM)
SMEM = pl.BlockSpec(memory_space=pltpu.SMEM)
HBM = pl.BlockSpec(memory_space=pltpu.HBM)
CHUNKS = 4
HALVES = 2
ROWS = 16
PARAMS = pltpu.CompilerParams(vmem_limit_bytes=24 * 2**20)


def kernel_tables(count):
    index = np.arange(count, dtype=np.float64)
    offset = index[:, None] - index[None, :]
    smooth = np.exp(-offset * offset / (2.0 * sigma_spot * sigma_spot)) / (
        2.5066282746310002 * sigma_spot
    )
    smooth = np.where(np.abs(offset) < 4.0 * sigma_spot, smooth, 0.0)
    curve = (offset * offset / sigma_spot**4 - 1.0 / sigma_spot**2) * smooth
    return smooth, curve


def plane_tables(depth, height):
    gauss_z, curve_z = kernel_tables(depth)
    gauss_y, curve_y = kernel_tables(height)
    factor = -(sigma_spot * sigma_spot)
    with_bent = np.kron(gauss_z, gauss_y)
    with_smooth = np.kron(gauss_z, curve_y) + np.kron(curve_z, gauss_y)
    table = (factor * np.concatenate([with_bent, with_smooth], axis=0)).astype(np.float32)
    high = table.astype(BF)
    low = (table - high.astype(np.float32)).astype(BF)
    return np.concatenate([high, low], axis=0)


def line_tables(width):
    gauss_x, curve_x = kernel_tables(width)
    return np.stack([np.tile(t.T, (2, 1)) for t in (curve_x, gauss_x)]).astype(np.float32)


def lanes_of(shape):
    return lax.broadcasted_iota(jnp.int32, shape, len(shape) - 1)


def pack(valid_ref, img_ref, is_tail):
    bricks, channels, plane, width = img_ref.shape
    slot = width // channels
    first = lax.axis_index("brick") * bricks
    lane = lanes_of((plane, width))
    brick = jnp.where(is_tail, bricks - 1, 0)
    at = jnp.where(is_tail, width - slot, 0)
    row = jnp.zeros((plane, width), F32)
    for c in range(channels):
        data = img_ref[brick, c].astype(F32)
        moved = pltpu.roll(data, lax.rem(c * slot + width - at, width), 1)
        row = jnp.where(lane // slot == c, moved, row)
    return (row * valid_ref[first + brick].astype(F32)).astype(BF)


def swaps_of(count):
    both = lambda couples: [link for a, b in couples for link in ((a, b), (b, a))]
    even = both([(i, i + 1) for i in range(0, count - 1, 2)])
    if count % 4 or count < 8:
        return [even, both([(i, i + 1) for i in range(1, count - 1, 2)])]
    second = both([(i + 1, i + 2) for i in range(0, count, 4)] + [(i, i + 3) for i in range(0, count, 4)])
    third = both([(i, i + 1) for i in range(3, count - 1, 4)] + [(i, i + 1) for i in range(5, count - 4, 4)])
    for a, b, c in ((0, 1, 2), (count - 3, count - 2, count - 1)):
        third += [(a, b), (b, c), (c, a)]
    return [even, second, third]


class Filter:
    def __init__(self, shift_ref, frac_ref, valid_ref, img_ref, plane_ref=None, line_ref=None, halo=()):
        self.shift, self.frac, self.valid = shift_ref, frac_ref, valid_ref
        self.img, self.plane, self.line, self.halo = img_ref, plane_ref, line_ref, halo

    def valid_of(self, b):
        return self.valid[lax.axis_index("brick") * self.shift.shape[1] + b].astype(F32)

    def field(self, b):
        bricks = self.shift.shape[1]
        _, channels, plane, width = self.img.shape
        slot = width // channels
        tiles = (plane // 8, 8, width)
        lane = lanes_of((8, width))
        s = self.shift[0, b]
        f = self.frac[0, b]
        right = s >= 0
        nb = jnp.where(right, b - 1, b + 1)
        nb_in = jnp.clip(nb, 0, bricks - 1)
        first = lax.axis_index("brick") * bricks
        own_valid = self.valid_of(b)
        nb_valid = self.valid_of(nb_in)
        if self.halo:
            there_is = jnp.logical_and(first + nb >= 0, first + nb < self.valid.shape[0])
            nb_valid = jnp.where(nb == nb_in, nb_valid, there_is.astype(F32))
            index = lax.axis_index("brick")
            in_first = (nb < 0) == (lax.rem(index, 2) == 1)
            second, third = self.halo[1], self.halo[-1]
            in_second = lax.rem(index, 4) % 3 != 0
            halo = jnp.where(in_second, second[...], third[...])
            halo = jnp.where(in_first, self.halo[0][...], halo).astype(F32).reshape(tiles)
            start = jnp.where(nb < 0, width - slot, 0)
        low0, high0 = jnp.where(right, 0, -s), jnp.where(right, width - s, width)
        low1, high1 = jnp.where(right, 0, -s - 1), jnp.where(right, width - s - 1, width)
        own0 = (lane >= low0) & (lane < high0)
        own1 = (lane >= low1) & (lane < high1)
        gain0 = (1.0 - f) * jnp.where(own0, own_valid, nb_valid)
        gain1 = f * jnp.where(own1, own_valid, nb_valid)
        own0, own1 = (jnp.broadcast_to(m, tiles) for m in (own0, own1))
        parts = []
        for c in range(channels):
            own = self.img[b, c].astype(F32).reshape(tiles)
            other = self.img[nb_in, c].astype(F32).reshape(tiles)
            if self.halo:
                moved = pltpu.roll(halo, lax.rem(start + (width - c * slot), width), 2)
                other = jnp.where(nb == nb_in, other, moved)
            here = jnp.where(own0, own, other) * gain0
            there = jnp.where(own1, own, other) * gain1
            value = (here + pltpu.roll(there, 1, 2)).reshape(plane, width).astype(BF)
            parts.append(value)
        return parts

    def weights(self, b):
        width = self.img.shape[-1]
        s = self.shift[0, b]
        f = self.frac[0, b]
        right = s >= 0
        own_valid = self.valid_of(b)
        nb_valid = self.valid_of(jnp.where(right, b - 1, b + 1))
        row = lax.broadcasted_iota(jnp.int32, (width, width), 0)
        lane = lanes_of((width, width))
        mine, theirs = jnp.zeros((width, width), F32), jnp.zeros((width, width), F32)
        for step, gain in ((s, 1.0 - f), (s + 1, f)):
            low, high = jnp.where(right, 0, -step), jnp.where(right, width - step, width)
            inside = (row >= low) & (row < high)
            to = row + step
            to = jnp.where(to < 0, to + width, jnp.where(to >= width, to - width, to))
            mine = mine + jnp.where(inside & (to == lane), gain * own_valid, 0.0)
            theirs = theirs + jnp.where(jnp.logical_not(inside) & (to == lane), gain * nb_valid, 0.0)
        table = jnp.concatenate([mine, theirs], axis=0)
        high = table.astype(BF)
        low = (table - high.astype(F32)).astype(BF)
        return jnp.concatenate([high, low], axis=1)

    def turn_of(self, b):
        s = self.shift[0, b]
        return jnp.where(s < 0, s + self.img.shape[-1], s)

    def apply(self, parts, turn, put, totals, weight):
        plane, width = parts[0].shape
        field = jnp.concatenate(parts, axis=1)
        dot = functools.partial(jnp.dot, preferred_element_type=F32)
        half = 2 * plane
        mixed = dot(self.plane[:half], field) + dot(self.plane[half:], field)
        line = jnp.concatenate([self.line[k, pl.ds(turn, width), :] for k in range(2)], axis=0)
        line_high = line.astype(BF)
        line_low = (line - line_high.astype(F32)).astype(BF)
        lines = jnp.concatenate([line_high, line_low], axis=1)
        added = []
        for c, total in enumerate(totals):
            wide = jnp.concatenate(
                [mixed[k * plane : (k + 1) * plane, c * width : (c + 1) * width] for k in range(2)],
                axis=1,
            )
            both = dot(wide.astype(BF), lines)
            result = (both[:, :width] + both[:, width:]).astype(BF)
            put(c, result)
            size = jnp.abs(result.astype(F32)).reshape(plane // 8, 8, width)
            added.append(total + jnp.sum(size, axis=0) * weight)
        return added

    def __call__(self, b, put, totals):
        parts = self.field(b)
        return self.apply(parts, self.turn_of(b), put, totals, self.valid_of(b))


def put_in(refs, n):
    def put(c, value):
        rows = value.shape[0] // len(refs)
        for k, ref in enumerate(refs):
            ref[n, c] = value[k * rows : (k + 1) * rows]

    return put


def load_kernel(picks, shift_hbm, frac_hbm, valid_hbm, img_ref, *refs):
    part_refs, refs = refs[: len(picks)], refs[len(picks) :]
    shift_ref, frac_ref, valid_ref, near_ref, near_sem, small_sem = refs
    bricks = img_ref.shape[0]
    rank = lax.axis_index("round")
    pairs = [(shift_hbm, shift_ref), (frac_hbm, frac_ref), (valid_hbm, valid_ref)]
    copies = [pltpu.make_async_copy(a, b, small_sem.at[n]) for n, (a, b) in enumerate(pairs)]
    bases = [pick(rank) - 1 for pick in picks]
    for k, base in enumerate(bases):
        for n in range(3):
            b = jnp.clip(base + n, 0, bricks - 1)
            copies.append(pltpu.make_async_copy(img_ref.at[b], near_ref.at[3 * k + n], near_sem.at[3 * k + n]))
    for copy in copies:
        copy.start()
    for copy in copies[:3]:
        copy.wait()
    one = Filter(shift_ref, frac_ref, valid_ref, near_ref)
    weights = [one.weights(base + 1) for base in bases]
    for copy in copies[3:]:
        copy.wait()
    for k, (base, part_ref) in enumerate(zip(bases, part_refs, strict=True)):
        side = jnp.where(shift_ref[0, base + 1] >= 0, 0, 2)
        for c in range(img_ref.shape[1]):
            both = jnp.concatenate([near_ref[3 * k + 1, c], near_ref[3 * k + side, c]], axis=1)
            terms = jnp.dot(both, weights[k], preferred_element_type=F32)
            width = terms.shape[1] // 2
            part_ref[0, c] = (terms[:, :width] + terms[:, width:]).astype(BF)


def pack_kernel(valid_ref, img_ref, swap0_ref, swap1_ref):
    even = lax.rem(lax.axis_index("brick"), 2) == 0
    swap0_ref[...] = pack(valid_ref, img_ref, even)
    swap1_ref[...] = pack(valid_ref, img_ref, jnp.logical_not(even))


def filter_kernel(groups, first, edge, ahead, behind, shift_ref, frac_ref, valid_ref, img_ref, plane_ref, line_ref, *refs):
    sums_ref = None
    halo, refs = refs[:edge], refs[edge:]
    if not first:
        sums_ref, refs = refs[0], refs[1:]
    if behind:
        field_ref, refs = refs[0], refs[1:]
    *out_refs, stat_ref = refs
    if ahead:
        *out_refs, next_ref = out_refs
    _, channels, _, width = img_ref.shape
    rank = lax.axis_index("round")
    one = Filter(shift_ref, frac_ref, valid_ref, img_ref, plane_ref, line_ref, halo)
    totals = [jnp.zeros((8, width), F32) if first else sums_ref[c] for c in range(channels)]
    for picks, halves in groups:
        refs, out_refs = out_refs[:halves], out_refs[halves:]
        for n, pick in enumerate(picks):
            b = pick(rank)
            if behind:
                parts = [field_ref[c] for c in range(channels)]
                totals = one.apply(parts, one.turn_of(b), put_in(refs, n), totals, one.valid_of(b))
            else:
                totals = one(b, put_in(refs, n), totals)
            behind = False
    if ahead:
        for c, part in enumerate(one.field(ahead(rank))):
            next_ref[c] = part
    for c in range(channels):
        stat_ref[c] = totals[c]


def close_kernel(pick, shift_ref, frac_ref, valid_ref, plane_ref, line_ref, sums_ref, *refs):
    *refs, stat_ref = refs
    peers = len(refs) // 2
    part_refs, out_refs = refs[:peers], refs[peers:]
    channels, _, width = sums_ref.shape
    rank = lax.axis_index("round")
    one = Filter(shift_ref, frac_ref, valid_ref, None, plane_ref, line_ref)
    found = [sums_ref[c] for c in range(channels)]
    for part_ref, out_ref in zip(part_refs, out_refs, strict=True):
        parts = [part_ref[0, c] for c in range(channels)]
        totals = [jnp.zeros((8, width), F32) for _ in range(channels)]
        found += one.apply(parts, 0, put_in([out_ref], 0), totals, one.valid_of(pick(rank)))
    packed = jnp.zeros(stat_ref.shape[1:], F32)
    for n, total in enumerate(found):
        packed = jnp.where(lanes_of(packed.shape) == n, jnp.sum(total), packed)
    stat_ref[...] = jnp.broadcast_to(packed, stat_ref.shape)


def norm_kernel(rounds, tasks, out_ref, inverse_ref, data_refs, buf_refs, kept_ref, sem):
    _, channels, plane, width = out_ref.shape[2:]
    step = plane // CHUNKS
    tiles = (ROWS // 8, 8, width)
    copies = []
    stored, kept = 0, 0
    for j, n, sources, keep in tasks:
        to_ref, m = (kept_ref, kept) if keep else (buf_refs, stored)
        for first in range(0, step, ROWS):
            ratios = []
            energy = jnp.zeros(tiles, F32)
            for d in range(rounds):
                g, k, base = sources[d]
                begin = n * step - base + first
                for c in range(channels):
                    data = data_refs[g][k, c, begin : begin + ROWS]
                    ratio = data.astype(F32).reshape(tiles) * inverse_ref[d, c]
                    energy = energy + ratio * ratio
                    ratios.append(ratio)
            factor = lax.rsqrt(energy * (1.0 / (rounds * channels)) + 1.0)
            for d in range(rounds):
                for c in range(channels):
                    value = (ratios[d * channels + c] * factor).reshape(ROWS, width).astype(BF)
                    to_ref[m, d, c, first : first + ROWS] = value
        if keep:
            kept += 1
        else:
            copies += store(rounds, j, n, buf_refs.at[m], out_ref, sem.at[m])
            stored += 1
    return copies


def store(rounds, j, n, from_ref, out_ref, sem):
    quota, _, plane, _ = out_ref.shape[2:]
    rank = lax.axis_index("round")
    pos = jnp.where(rank == 0, quota - 1 - j, j)
    step = plane // CHUNKS
    copies = []
    for d in range(rounds):
        slot = lax.rem(rank + rounds - d, rounds)
        to_ref = out_ref.at[slot, 0, pos, :, pl.ds(n * step, step)]
        copy = pltpu.make_async_copy(from_ref.at[d], to_ref, sem.at[d])
        copy.start()
        copies.append(copy)
    return copies


def norm1_kernel(rounds, shared, tasks, valid_ref, stat_ref, *refs):
    *data_refs, out_ref, inverse_ref, kept_ref, buf_ref, sem = refs
    _, channels, plane, width = out_ref.shape[2:]
    rank = lax.axis_index("round")
    count = jnp.maximum(jnp.sum(valid_ref[...]).astype(F32), 1.0)
    each = stat_ref.shape[0] // rounds
    sums = [jnp.sum(stat_ref[q * each : (q + 1) * each], axis=0) for q in range(rounds)]
    wide = {
        (q, e, c): jnp.broadcast_to(sums[q][:, e * channels + c : e * channels + c + 1], (8, width))
        for q in range(rounds)
        for e in range(rounds if shared else 1)
        for c in range(channels)
    }
    for d in range(rounds):
        slot = lax.rem(rank + rounds - d, rounds)
        for c in range(channels):
            total = jnp.zeros((8, width), F32)
            for q in range(rounds):
                of_round = functools.reduce(
                    jnp.add, [wide[(q + e) % rounds, e, c] for e in range(rounds if shared else 1)]
                )
                total = jnp.where(slot == q, of_round, total)
            inverse_ref[d, c] = 1.0 / (total / (count * (plane * width)) + 1e-06)
    for copy in norm_kernel(rounds, tasks, out_ref, inverse_ref, data_refs, buf_ref, kept_ref, sem):
        copy.wait()


def norm2_kernel(rounds, tasks, carried, result_ref, inverse_ref, kept_ref, *refs):
    *data_refs, out_ref, buf_ref, sem, kept_sem = refs
    copies = []
    for m, (j, n) in enumerate(carried):
        copies += store(rounds, j, n, kept_ref.at[m], out_ref, kept_sem.at[m])
    copies += norm_kernel(rounds, tasks, out_ref, inverse_ref, data_refs, buf_ref, None, sem)
    for copy in copies:
        copy.wait()


def in_vmem(x):
    return pltpu.with_memory_space_constraint(x, pltpu.VMEM)


def in_smem(x):
    return pltpu.with_memory_space_constraint(x, pltpu.SMEM)


def in_hbm(x):
    return pltpu.with_memory_space_constraint(x, pltpu.HBM)


def body(image, shifts, fractions, valid):
    _, bricks, channels, depth, height, width = image.shape
    plane = depth * height
    rounds = lax.axis_size("round")
    count = lax.axis_size("brick")
    quota = bricks // rounds
    img = image.reshape(bricks, channels, plane, width)
    plane_table = jnp.asarray(plane_tables(depth, height))
    line_table = jnp.asarray(line_tables(width))

    def out(shape, dtype):
        return pltpu.VMEM(shape, dtype)

    def pick_for(d, j):
        def pick(rank):
            target = lax.rem(rank + d, rounds)
            return target * quota + jnp.where(target == 0, quota - 1 - j, j)

        return pick

    peers = range(1, rounds)
    early = [0] if quota > 1 else []
    inner = list(range(1, quota - 1))
    sum_shape = out((channels, 8, width), F32)
    firsts = [pick_for(d, 0) for d in peers] if early else []
    sources = [shifts, fractions, valid]

    *parts, shift_s, frac_s, valid_s = pl.pallas_call(
        functools.partial(load_kernel, firsts),
        in_specs=[HBM] * 4,
        out_specs=[VMEM] * len(firsts) + [SMEM] * 3,
        out_shape=[out((1, channels, plane, width), BF)] * len(firsts)
        + [pltpu.SMEM(a.shape, a.dtype) for a in sources],
        scratch_shapes=[
            pltpu.VMEM((3 * max(len(firsts), 1), channels, plane, width), BF),
            pltpu.SemaphoreType.DMA((3 * max(len(firsts), 1),)),
            pltpu.SemaphoreType.DMA((3,)),
        ],
        name="load",
        compiler_params=PARAMS,
    )(*[in_hbm(a) for a in (*sources, img)])
    scalars = [in_smem(a) for a in (shift_s, frac_s, valid_s)]
    tables = [in_vmem(a) for a in (plane_table, line_table)]

    def send(parts):
        chunks = []
        for d, part in zip(peers, parts, strict=True):
            chunks.append(lax.ppermute(part, "round", [(i, (i + d) % rounds) for i in range(rounds)]))
        return chunks

    def filtered(groups, sums, halo=(), ahead=None, field=()):
        ins = [in_vmem(img), *tables, *[in_vmem(a) for a in (*halo, *sums, *field)]]
        return pl.pallas_call(
            functools.partial(filter_kernel, groups, not sums, len(halo), ahead, bool(field)),
            in_specs=[SMEM] * 3 + [VMEM] * len(ins),
            out_specs=[VMEM] * (sum(halves for _, halves in groups) + bool(ahead) + 1),
            out_shape=[
                out((len(g), channels, plane // halves, width), BF) for g, halves in groups for _ in range(halves)
            ]
            + [out(img.shape[1:], BF)] * bool(ahead)
            + [sum_shape],
            compiler_params=PARAMS,
        )(*scalars, *ins)

    shifted = send(parts) if early else []
    swaps = pl.pallas_call(
        pack_kernel,
        in_specs=[SMEM, VMEM],
        out_specs=[VMEM] * 2,
        out_shape=[out((plane, width), BF)] * 2,
        name="pack",
        compiler_params=PARAMS,
    )(scalars[2], in_vmem(img))
    halo = []
    for links, swap in zip(swaps_of(count), (swaps[0], swaps[1], swaps[1])):
        halo.append(lax.ppermute(swap, "brick", links))
    sums, fields = [], []
    if inner:
        groups = [([pick_for(d, j) for j in inner], 1) for d in peers]
        *parts, field, stat = filtered(groups, sums, ahead=pick_for(0, 0))
        fields = [field]
        sums = [stat]
        arrived_inner = send(parts)
    last = quota - 1
    if last:
        own, stat = filtered([([pick_for(0, j) for j in range(last)], 1)], sums, field=fields)
        sums = [stat]
    groups = [([pick_for(0, last)], 1)] + [([pick_for(d, last)], HALVES) for d in peers]
    own_last, *parts, stat = filtered(groups, sums, halo)
    ins = [*tables, *[in_vmem(a) for a in (stat, *shifted)]]
    *arrived, stat = pl.pallas_call(
        functools.partial(close_kernel, pick_for(0, 0)),
        in_specs=[SMEM] * 3 + [VMEM] * len(ins),
        out_specs=[VMEM] * (len(shifted) + 1),
        out_shape=[out((1, channels, plane, width), BF)] * len(shifted)
        + [jax.ShapeDtypeStruct((rounds * count, 1, width), F32)],
        name="k4",
        compiler_params=PARAMS,
    )(*scalars, *ins)
    stats = lax.all_to_all(stat, ("round", "brick"), split_axis=0, concat_axis=0, tiled=True)

    arrived_last = [send(parts[k::HALVES]) for k in range(HALVES)]

    part = plane // HALVES
    step = plane // CHUNKS

    def task(j, n, keep, arrays):
        if j < last:
            theirs = arrived if j == 0 else arrived_inner
            found = [(own, j, 0)] + [(a, 0 if j == 0 else j - 1, 0) for a in theirs]
        else:
            k = n * step // part
            found = [(own_last, 0, 0)] + [(a, 0, k * part) for a in arrived_last[k]]
        sources = []
        for array, m, base in found:
            if all(array is not a for a in arrays):
                arrays.append(array)
            sources.append(([array is a for a in arrays].index(True), m, base))
        return j, n, sources, keep

    pieces = [(j, n) for j in range(quota) for n in range(CHUNKS)]
    late = pieces[len(pieces) - CHUNKS // HALVES :]
    pieces = pieces[: len(pieces) - len(late)]
    carried = pieces[len(pieces) * 5 // 7 :]
    arrays = []
    tasks = [task(j, n, (j, n) in carried, arrays) for j, n in pieces]
    tile = (rounds, channels, step, width)
    ins = [in_vmem(a) for a in (valid.reshape(1, -1), stats, *arrays)]
    stored = max(len(pieces) - len(carried), 1)
    result, inverse, kept = pl.pallas_call(
        functools.partial(norm1_kernel, rounds, bool(early), tasks),
        in_specs=[VMEM] * len(ins),
        out_specs=[HBM, VMEM, VMEM],
        out_shape=[
            jax.ShapeDtypeStruct((rounds, 1, quota, channels, plane, width), BF),
            out((rounds, channels, 8, width), F32),
            out((len(carried), *tile), BF),
        ],
        scratch_shapes=[pltpu.VMEM((stored, *tile), BF), pltpu.SemaphoreType.DMA((stored, rounds))],
        name="norm1",
        compiler_params=PARAMS,
    )(*ins)
    arrays = []
    tasks = [task(j, n, False, arrays) for j, n in late]
    ins = [in_hbm(result)] + [in_vmem(a) for a in (inverse, kept, *arrays)]
    result = pl.pallas_call(
        functools.partial(norm2_kernel, rounds, tasks, carried),
        in_specs=[HBM] + [VMEM] * (len(ins) - 1),
        out_specs=HBM,
        out_shape=jax.ShapeDtypeStruct(result.shape, BF),
        scratch_shapes=[
            pltpu.VMEM((len(late), *tile), BF),
            pltpu.SemaphoreType.DMA((len(late), rounds)),
            pltpu.SemaphoreType.DMA((len(carried), rounds)),
        ],
        input_output_aliases={0: 0},
        name="norm2",
        compiler_params=PARAMS,
    )(*ins)
    return result.reshape(rounds, 1, quota, channels, depth, height, width)


def solution(mesh):
    in_specs = (
        P("round", "brick", None, None, None, None),
        P("round", "brick"),
        P("round", "brick"),
        P(),
    )
    out_specs = P(None, "round", "brick", None, None, None, None)
    return jax.shard_map(body, mesh=mesh, in_specs=in_specs, out_specs=out_specs, check_vma=False)
```

```python
import functools

import jax
import jax.numpy as jnp
import numpy as np
from jax import lax
from jax.experimental import pallas as pl
from jax.experimental.pallas import tpu as pltpu
from jax.sharding import PartitionSpec as P

sigma_spot = 1.5


BF = jnp.bfloat16
F32 = jnp.float32
VMEM = pl.BlockSpec(memory_space=pltpu.VMEM)
SMEM = pl.BlockSpec(memory_space=pltpu.SMEM)
HBM = pl.BlockSpec(memory_space=pltpu.HBM)
CHUNKS = 4
HALVES = 2
ROWS = 16
PARAMS = pltpu.CompilerParams(vmem_limit_bytes=24 * 2**20)


def kernel_tables(count):
    index = np.arange(count, dtype=np.float64)
    offset = index[:, None] - index[None, :]
    smooth = np.exp(-offset * offset / (2.0 * sigma_spot * sigma_spot)) / (
        2.5066282746310002 * sigma_spot
    )
    smooth = np.where(np.abs(offset) < 4.0 * sigma_spot, smooth, 0.0)
    curve = (offset * offset / sigma_spot**4 - 1.0 / sigma_spot**2) * smooth
    return smooth, curve


def plane_tables(depth, height):
    gauss_z, curve_z = kernel_tables(depth)
    gauss_y, curve_y = kernel_tables(height)
    factor = -(sigma_spot * sigma_spot)
    with_bent = np.kron(gauss_z, gauss_y)
    with_smooth = np.kron(gauss_z, curve_y) + np.kron(curve_z, gauss_y)
    table = (factor * np.concatenate([with_bent, with_smooth], axis=0)).astype(np.float32)
    high = table.astype(BF)
    low = (table - high.astype(np.float32)).astype(BF)
    return np.concatenate([high, low], axis=0)


def line_tables(width):
    gauss_x, curve_x = kernel_tables(width)
    return np.stack([np.tile(t.T, (2, 1)) for t in (curve_x, gauss_x)]).astype(np.float32)


def lanes_of(shape):
    return lax.broadcasted_iota(jnp.int32, shape, len(shape) - 1)


def pack(valid_ref, img_ref, is_tail):
    bricks, channels, plane, width = img_ref.shape
    slot = width // channels
    first = lax.axis_index("brick") * bricks
    lane = lanes_of((plane, width))
    brick = jnp.where(is_tail, bricks - 1, 0)
    at = jnp.where(is_tail, width - slot, 0)
    row = jnp.zeros((plane, width), F32)
    for c in range(channels):
        data = img_ref[brick, c].astype(F32)
        moved = pltpu.roll(data, lax.rem(c * slot + width - at, width), 1)
        row = jnp.where(lane // slot == c, moved, row)
    return (row * valid_ref[first + brick].astype(F32)).astype(BF)


def swaps_of(count):
    both = lambda couples: [link for a, b in couples for link in ((a, b), (b, a))]
    even = both([(i, i + 1) for i in range(0, count - 1, 2)])
    if count % 4 or count < 8:
        return [even, both([(i, i + 1) for i in range(1, count - 1, 2)])]
    second = both([(i + 1, i + 2) for i in range(0, count, 4)] + [(i, i + 3) for i in range(0, count, 4)])
    third = both([(i, i + 1) for i in range(3, count - 1, 4)] + [(i, i + 1) for i in range(5, count - 4, 4)])
    for a, b, c in ((0, 1, 2), (count - 3, count - 2, count - 1)):
        third += [(a, b), (b, c), (c, a)]
    return [even, second, third]


class Filter:
    def __init__(self, shift_ref, frac_ref, valid_ref, img_ref, plane_ref=None, line_ref=None, halo=()):
        self.shift, self.frac, self.valid = shift_ref, frac_ref, valid_ref
        self.img, self.plane, self.line, self.halo = img_ref, plane_ref, line_ref, halo

    def valid_of(self, b):
        return self.valid[lax.axis_index("brick") * self.shift.shape[1] + b].astype(F32)

    def field(self, b, at, turned):
        bricks = self.shift.shape[1]
        _, channels, plane, width = self.img.shape
        slot = width // channels
        tiles = (plane // 8, 8, width)
        lane = lanes_of((8, width))
        s = self.shift[0, b]
        f = self.frac[0, b]
        right = s >= 0
        nb = jnp.where(right, b - 1, b + 1)
        nb_in = jnp.clip(nb, 0, bricks - 1)
        first = lax.axis_index("brick") * bricks
        own_valid = self.valid_of(b)
        nb_valid = self.valid_of(nb_in)
        if self.halo:
            there_is = jnp.logical_and(first + nb >= 0, first + nb < self.valid.shape[0])
            nb_valid = jnp.where(nb == nb_in, nb_valid, there_is.astype(F32))
            index = lax.axis_index("brick")
            in_first = (nb < 0) == (lax.rem(index, 2) == 1)
            second, third = self.halo[1], self.halo[-1]
            in_second = lax.rem(index, 4) % 3 != 0
            halo = jnp.where(in_second, second[...], third[...])
            halo = jnp.where(in_first, self.halo[0][...], halo).astype(F32).reshape(tiles)
            start = jnp.where(nb < 0, width - slot, 0)
        low0, high0 = jnp.where(right, 0, -s), jnp.where(right, width - s, width)
        low1, high1 = jnp.where(right, 0, -s - 1), jnp.where(right, width - s - 1, width)
        own0 = (lane >= low0) & (lane < high0)
        own1 = (lane >= low1) & (lane < high1)
        gain0 = (1.0 - f) * jnp.where(own0, own_valid, nb_valid)
        gain1 = f * jnp.where(own1, own_valid, nb_valid)
        own0, own1 = (jnp.broadcast_to(m, tiles) for m in (own0, own1))
        if turned:
            row = lax.broadcasted_iota(jnp.int32, (width, width), 0) + self.turn_of(b)
            row = jnp.where(row >= width, row - width, row)
            turn = (row == lanes_of((width, width))).astype(F32).astype(BF)
        parts = []
        for c in range(channels):
            own = self.img[at(b), c].astype(F32).reshape(tiles)
            other = self.img[at(nb_in), c].astype(F32).reshape(tiles)
            if self.halo:
                moved = pltpu.roll(halo, lax.rem(start + (width - c * slot), width), 2)
                other = jnp.where(nb == nb_in, other, moved)
            here = jnp.where(own0, own, other) * gain0
            there = jnp.where(own1, own, other) * gain1
            value = (here + pltpu.roll(there, 1, 2)).reshape(plane, width).astype(BF)
            if turned:
                value = jnp.dot(value, turn, preferred_element_type=F32).astype(BF)
            parts.append(value)
        return parts

    def turn_of(self, b):
        s = self.shift[0, b]
        return jnp.where(s < 0, s + self.img.shape[-1], s)

    def apply(self, parts, turn, put, totals, weight):
        plane, width = parts[0].shape
        field = jnp.concatenate(parts, axis=1)
        dot = functools.partial(jnp.dot, preferred_element_type=F32)
        half = 2 * plane
        mixed = dot(self.plane[:half], field) + dot(self.plane[half:], field)
        line = jnp.concatenate([self.line[k, pl.ds(turn, width), :] for k in range(2)], axis=0)
        line_high = line.astype(BF)
        line_low = (line - line_high.astype(F32)).astype(BF)
        lines = jnp.concatenate([line_high, line_low], axis=1)
        added = []
        for c, total in enumerate(totals):
            wide = jnp.concatenate(
                [mixed[k * plane : (k + 1) * plane, c * width : (c + 1) * width] for k in range(2)],
                axis=1,
            )
            both = dot(wide.astype(BF), lines)
            result = (both[:, :width] + both[:, width:]).astype(BF)
            put(c, result)
            size = jnp.abs(result.astype(F32)).reshape(plane // 8, 8, width)
            added.append(total + jnp.sum(size, axis=0) * weight)
        return added

    def __call__(self, b, put, totals):
        parts = self.field(b, lambda n: n, False)
        return self.apply(parts, self.turn_of(b), put, totals, self.valid_of(b))


def put_in(refs, n):
    def put(c, value):
        rows = value.shape[0] // len(refs)
        for k, ref in enumerate(refs):
            ref[n, c] = value[k * rows : (k + 1) * rows]

    return put


def load_kernel(picks, shift_hbm, frac_hbm, valid_hbm, img_ref, *refs):
    part_refs, refs = refs[: len(picks)], refs[len(picks) :]
    shift_ref, frac_ref, valid_ref, near_ref, near_sem, small_sem = refs
    bricks = img_ref.shape[0]
    rank = lax.axis_index("round")
    pairs = [(shift_hbm, shift_ref), (frac_hbm, frac_ref), (valid_hbm, valid_ref)]
    copies = [pltpu.make_async_copy(a, b, small_sem.at[n]) for n, (a, b) in enumerate(pairs)]
    bases = [pick(rank) - 1 for pick in picks]
    for k, base in enumerate(bases):
        for n in range(3):
            b = jnp.clip(base + n, 0, bricks - 1)
            copies.append(pltpu.make_async_copy(img_ref.at[b], near_ref.at[3 * k + n], near_sem.at[3 * k + n]))
    for copy in copies:
        copy.start()
    for copy in copies:
        copy.wait()
    one = Filter(shift_ref, frac_ref, valid_ref, near_ref)
    for k, (base, part_ref) in enumerate(zip(bases, part_refs, strict=True)):
        parts = one.field(base + 1, lambda n, k=k, base=base: n - base + 3 * k, True)
        for c, part in enumerate(parts):
            part_ref[0, c] = part


def pack_kernel(valid_ref, img_ref, swap0_ref, swap1_ref):
    even = lax.rem(lax.axis_index("brick"), 2) == 0
    swap0_ref[...] = pack(valid_ref, img_ref, even)
    swap1_ref[...] = pack(valid_ref, img_ref, jnp.logical_not(even))


def filter_kernel(groups, first, edge, ahead, behind, shift_ref, frac_ref, valid_ref, img_ref, plane_ref, line_ref, *refs):
    sums_ref = None
    halo, refs = refs[:edge], refs[edge:]
    if not first:
        sums_ref, refs = refs[0], refs[1:]
    if behind:
        field_ref, refs = refs[0], refs[1:]
    *out_refs, stat_ref = refs
    if ahead:
        *out_refs, next_ref = out_refs
    _, channels, _, width = img_ref.shape
    rank = lax.axis_index("round")
    one = Filter(shift_ref, frac_ref, valid_ref, img_ref, plane_ref, line_ref, halo)
    totals = [jnp.zeros((8, width), F32) if first else sums_ref[c] for c in range(channels)]
    for picks, halves in groups:
        refs, out_refs = out_refs[:halves], out_refs[halves:]
        for n, pick in enumerate(picks):
            b = pick(rank)
            if behind:
                parts = [field_ref[c] for c in range(channels)]
                totals = one.apply(parts, one.turn_of(b), put_in(refs, n), totals, one.valid_of(b))
            else:
                totals = one(b, put_in(refs, n), totals)
            behind = False
    if ahead:
        for c, part in enumerate(one.field(ahead(rank), lambda n: n, False)):
            next_ref[c] = part
    for c in range(channels):
        stat_ref[c] = totals[c]


def close_kernel(pick, shift_ref, frac_ref, valid_ref, plane_ref, line_ref, sums_ref, *refs):
    *refs, stat_ref = refs
    peers = len(refs) // 2
    part_refs, out_refs = refs[:peers], refs[peers:]
    channels, _, width = sums_ref.shape
    rank = lax.axis_index("round")
    one = Filter(shift_ref, frac_ref, valid_ref, None, plane_ref, line_ref)
    found = [sums_ref[c] for c in range(channels)]
    for part_ref, out_ref in zip(part_refs, out_refs, strict=True):
        parts = [part_ref[0, c] for c in range(channels)]
        totals = [jnp.zeros((8, width), F32) for _ in range(channels)]
        found += one.apply(parts, 0, put_in([out_ref], 0), totals, one.valid_of(pick(rank)))
    packed = jnp.zeros(stat_ref.shape[1:], F32)
    for n, total in enumerate(found):
        packed = jnp.where(lanes_of(packed.shape) == n, jnp.sum(total), packed)
    stat_ref[...] = jnp.broadcast_to(packed, stat_ref.shape)


def norm_kernel(rounds, tasks, out_ref, inverse_ref, data_refs, buf_refs, kept_ref, sem):
    _, channels, plane, width = out_ref.shape[2:]
    step = plane // CHUNKS
    tiles = (ROWS // 8, 8, width)
    copies = []
    stored, kept = 0, 0
    for j, n, sources, keep in tasks:
        to_ref, m = (kept_ref, kept) if keep else (buf_refs, stored)
        for first in range(0, step, ROWS):
            ratios = []
            energy = jnp.zeros(tiles, F32)
            for d in range(rounds):
                g, k, base = sources[d]
                begin = n * step - base + first
                for c in range(channels):
                    data = data_refs[g][k, c, begin : begin + ROWS]
                    ratio = data.astype(F32).reshape(tiles) * inverse_ref[d, c]
                    energy = energy + ratio * ratio
                    ratios.append(ratio)
            factor = lax.rsqrt(energy * (1.0 / (rounds * channels)) + 1.0)
            for d in range(rounds):
                for c in range(channels):
                    value = (ratios[d * channels + c] * factor).reshape(ROWS, width).astype(BF)
                    to_ref[m, d, c, first : first + ROWS] = value
        if keep:
            kept += 1
        else:
            copies += store(rounds, j, n, buf_refs.at[m], out_ref, sem.at[m])
            stored += 1
    return copies


def store(rounds, j, n, from_ref, out_ref, sem):
    quota, _, plane, _ = out_ref.shape[2:]
    rank = lax.axis_index("round")
    pos = jnp.where(rank == 0, quota - 1 - j, j)
    step = plane // CHUNKS
    copies = []
    for d in range(rounds):
        slot = lax.rem(rank + rounds - d, rounds)
        to_ref = out_ref.at[slot, 0, pos, :, pl.ds(n * step, step)]
        copy = pltpu.make_async_copy(from_ref.at[d], to_ref, sem.at[d])
        copy.start()
        copies.append(copy)
    return copies


def norm1_kernel(rounds, shared, tasks, valid_ref, stat_ref, *refs):
    *data_refs, out_ref, inverse_ref, kept_ref, buf_ref, sem = refs
    _, channels, plane, width = out_ref.shape[2:]
    rank = lax.axis_index("round")
    count = jnp.maximum(jnp.sum(valid_ref[...]).astype(F32), 1.0)
    each = stat_ref.shape[0] // rounds
    sums = [jnp.sum(stat_ref[q * each : (q + 1) * each], axis=0) for q in range(rounds)]
    wide = {
        (q, e, c): jnp.broadcast_to(sums[q][:, e * channels + c : e * channels + c + 1], (8, width))
        for q in range(rounds)
        for e in range(rounds if shared else 1)
        for c in range(channels)
    }
    for d in range(rounds):
        slot = lax.rem(rank + rounds - d, rounds)
        for c in range(channels):
            total = jnp.zeros((8, width), F32)
            for q in range(rounds):
                of_round = functools.reduce(
                    jnp.add, [wide[(q + e) % rounds, e, c] for e in range(rounds if shared else 1)]
                )
                total = jnp.where(slot == q, of_round, total)
            inverse_ref[d, c] = 1.0 / (total / (count * (plane * width)) + 1e-06)
    for copy in norm_kernel(rounds, tasks, out_ref, inverse_ref, data_refs, buf_ref, kept_ref, sem):
        copy.wait()


def norm2_kernel(rounds, tasks, carried, result_ref, inverse_ref, kept_ref, *refs):
    *data_refs, out_ref, buf_ref, sem, kept_sem = refs
    copies = []
    for m, (j, n) in enumerate(carried):
        copies += store(rounds, j, n, kept_ref.at[m], out_ref, kept_sem.at[m])
    copies += norm_kernel(rounds, tasks, out_ref, inverse_ref, data_refs, buf_ref, None, sem)
    for copy in copies:
        copy.wait()


def in_vmem(x):
    return pltpu.with_memory_space_constraint(x, pltpu.VMEM)


def in_smem(x):
    return pltpu.with_memory_space_constraint(x, pltpu.SMEM)


def in_hbm(x):
    return pltpu.with_memory_space_constraint(x, pltpu.HBM)


def body(image, shifts, fractions, valid):
    _, bricks, channels, depth, height, width = image.shape
    plane = depth * height
    rounds = lax.axis_size("round")
    count = lax.axis_size("brick")
    quota = bricks // rounds
    img = image.reshape(bricks, channels, plane, width)
    plane_table = jnp.asarray(plane_tables(depth, height))
    line_table = jnp.asarray(line_tables(width))

    def out(shape, dtype):
        return pltpu.VMEM(shape, dtype)

    def pick_for(d, j):
        def pick(rank):
            target = lax.rem(rank + d, rounds)
            return target * quota + jnp.where(target == 0, quota - 1 - j, j)

        return pick

    peers = range(1, rounds)
    early = [0] if quota > 1 else []
    inner = list(range(1, quota - 1))
    sum_shape = out((channels, 8, width), F32)
    firsts = [pick_for(d, 0) for d in peers] if early else []
    sources = [shifts, fractions, valid]

    *parts, shift_s, frac_s, valid_s = pl.pallas_call(
        functools.partial(load_kernel, firsts),
        in_specs=[HBM] * 4,
        out_specs=[VMEM] * len(firsts) + [SMEM] * 3,
        out_shape=[out((1, channels, plane, width), BF)] * len(firsts)
        + [pltpu.SMEM(a.shape, a.dtype) for a in sources],
        scratch_shapes=[
            pltpu.VMEM((3 * max(len(firsts), 1), channels, plane, width), BF),
            pltpu.SemaphoreType.DMA((3 * max(len(firsts), 1),)),
            pltpu.SemaphoreType.DMA((3,)),
        ],
        name="load",
        compiler_params=PARAMS,
    )(*[in_hbm(a) for a in (*sources, img)])
    scalars = [in_smem(a) for a in (shift_s, frac_s, valid_s)]
    tables = [in_vmem(a) for a in (plane_table, line_table)]

    def send(parts):
        chunks = []
        for d, part in zip(peers, parts, strict=True):
            chunks.append(lax.ppermute(part, "round", [(i, (i + d) % rounds) for i in range(rounds)]))
        return chunks

    def filtered(groups, sums, halo=(), ahead=None, field=()):
        ins = [in_vmem(img), *tables, *[in_vmem(a) for a in (*halo, *sums, *field)]]
        return pl.pallas_call(
            functools.partial(filter_kernel, groups, not sums, len(halo), ahead, bool(field)),
            in_specs=[SMEM] * 3 + [VMEM] * len(ins),
            out_specs=[VMEM] * (sum(halves for _, halves in groups) + bool(ahead) + 1),
            out_shape=[
                out((len(g), channels, plane // halves, width), BF) for g, halves in groups for _ in range(halves)
            ]
            + [out(img.shape[1:], BF)] * bool(ahead)
            + [sum_shape],
            compiler_params=PARAMS,
        )(*scalars, *ins)

    shifted = send(parts) if early else []
    swaps = pl.pallas_call(
        pack_kernel,
        in_specs=[SMEM, VMEM],
        out_specs=[VMEM] * 2,
        out_shape=[out((plane, width), BF)] * 2,
        name="pack",
        compiler_params=PARAMS,
    )(scalars[2], in_vmem(img))
    halo = []
    for links, swap in zip(swaps_of(count), (swaps[0], swaps[1], swaps[1])):
        halo.append(lax.ppermute(swap, "brick", links))
    sums, fields = [], []
    if inner:
        groups = [([pick_for(d, j) for j in inner], 1) for d in peers]
        *parts, field, stat = filtered(groups, sums, ahead=pick_for(0, 0))
        fields = [field]
        sums = [stat]
        arrived_inner = send(parts)
    last = quota - 1
    if last:
        own, stat = filtered([([pick_for(0, j) for j in range(last)], 1)], sums, field=fields)
        sums = [stat]
    groups = [([pick_for(0, last)], 1)] + [([pick_for(d, last)], HALVES) for d in peers]
    own_last, *parts, stat = filtered(groups, sums, halo)
    ins = [*tables, *[in_vmem(a) for a in (stat, *shifted)]]
    *arrived, stat = pl.pallas_call(
        functools.partial(close_kernel, pick_for(0, 0)),
        in_specs=[SMEM] * 3 + [VMEM] * len(ins),
        out_specs=[VMEM] * (len(shifted) + 1),
        out_shape=[out((1, channels, plane, width), BF)] * len(shifted)
        + [jax.ShapeDtypeStruct((rounds * count, 1, width), F32)],
        name="k4",
        compiler_params=PARAMS,
    )(*scalars, *ins)
    stats = lax.all_to_all(stat, ("round", "brick"), split_axis=0, concat_axis=0, tiled=True)

    arrived_last = [send(parts[k::HALVES]) for k in range(HALVES)]

    part = plane // HALVES
    step = plane // CHUNKS

    def task(j, n, keep, arrays):
        if j < last:
            theirs = arrived if j == 0 else arrived_inner
            found = [(own, j, 0)] + [(a, 0 if j == 0 else j - 1, 0) for a in theirs]
        else:
            k = n * step // part
            found = [(own_last, 0, 0)] + [(a, 0, k * part) for a in arrived_last[k]]
        sources = []
        for array, m, base in found:
            if all(array is not a for a in arrays):
                arrays.append(array)
            sources.append(([array is a for a in arrays].index(True), m, base))
        return j, n, sources, keep

    pieces = [(j, n) for j in range(quota) for n in range(CHUNKS)]
    late = pieces[len(pieces) - CHUNKS // HALVES :]
    pieces = pieces[: len(pieces) - len(late)]
    carried = pieces[len(pieces) * 5 // 7 :]
    arrays = []
    tasks = [task(j, n, (j, n) in carried, arrays) for j, n in pieces]
    tile = (rounds, channels, step, width)
    ins = [in_vmem(a) for a in (valid.reshape(1, -1), stats, *arrays)]
    stored = max(len(pieces) - len(carried), 1)
    result, inverse, kept = pl.pallas_call(
        functools.partial(norm1_kernel, rounds, bool(early), tasks),
        in_specs=[VMEM] * len(ins),
        out_specs=[HBM, VMEM, VMEM],
        out_shape=[
            jax.ShapeDtypeStruct((rounds, 1, quota, channels, plane, width), BF),
            out((rounds, channels, 8, width), F32),
            out((len(carried), *tile), BF),
        ],
        scratch_shapes=[pltpu.VMEM((stored, *tile), BF), pltpu.SemaphoreType.DMA((stored, rounds))],
        name="norm1",
        compiler_params=PARAMS,
    )(*ins)
    arrays = []
    tasks = [task(j, n, False, arrays) for j, n in late]
    ins = [in_hbm(result)] + [in_vmem(a) for a in (inverse, kept, *arrays)]
    result = pl.pallas_call(
        functools.partial(norm2_kernel, rounds, tasks, carried),
        in_specs=[HBM] + [VMEM] * (len(ins) - 1),
        out_specs=HBM,
        out_shape=jax.ShapeDtypeStruct(result.shape, BF),
        scratch_shapes=[
            pltpu.VMEM((len(late), *tile), BF),
            pltpu.SemaphoreType.DMA((len(late), rounds)),
            pltpu.SemaphoreType.DMA((len(carried), rounds)),
        ],
        input_output_aliases={0: 0},
        name="norm2",
        compiler_params=PARAMS,
    )(*ins)
    return result.reshape(rounds, 1, quota, channels, depth, height, width)


def solution(mesh):
    in_specs = (
        P("round", "brick", None, None, None, None),
        P("round", "brick"),
        P("round", "brick"),
        P(),
    )
    out_specs = P(None, "round", "brick", None, None, None, None)
    return jax.shard_map(body, mesh=mesh, in_specs=in_specs, out_specs=out_specs, check_vma=False)
```
